256 devices in a mesh: seq: 8 (over y, core), exp: 32 (over z, x).
Axes of the slice: x: 4, y: 4, z: 8, core: 2. Of those that a mesh axis runs over, the one named last changes fastest.
Arguments:
- query_rows: bfloat16 [4096, 4096], P('seq', 'exp'), may hold values from -6 to 6
- key_rows: bfloat16 [4096, 4096], P('seq', 'exp'), may hold values from -6 to 6
- value_rows: bfloat16 [4096, 4096], P('seq', 'exp'), may hold values from -6 to 6
- output_gate: bfloat16 [4096, 4096], P('seq', 'exp'), may hold values from -6 to 6
- log_decay: float32 [32, 4096], P('exp', 'seq'), may hold values from -0.8 to 0
- write_rate: float32 [32, 4096], P('exp', 'seq'), may hold values from 0.001 to 1
- doc_start: int32 [4096], P('seq'), may hold values from 0 to 1, as said below
- state_in: float32 [32, 128, 128], P('exp'), may hold values from -6 to 6
- head_gain: float32 [128], replicated, may hold values from 0.5 to 1.5
- out_weight: bfloat16 [4096, 2048], P('exp'), may hold values from -0.09375 to 0.09375
- residual: bfloat16 [4096, 2048], P(('seq', 'exp')), may hold values from -6 to 6
- post_gain: float32 [2048], replicated, may hold values from 0.5 to 1.5
- expert_ids: int32 [4096, 10], P(('seq', 'exp')), may hold values from 0 to 255, all different within a row; in each aligned block of 16 rows (0 to 15, 16 to 31, ...) at most 2 rows name the same one
- expert_scale: float32 [4096, 10], P(('seq', 'exp')), may hold values from 0.02 to 0.2
- w_gate_up: bfloat16 [256, 2048, 1024], P(('seq', 'exp')), may hold values from -0.125 to 0.125
- w_down: bfloat16 [256, 512, 2048], P(('seq', 'exp')), may hold values from -0.25 to 0.25
Outputs:
- layer_out: bfloat16 [4096, 2048], P(('seq', 'exp'))
The draws below stay inside these ranges and needn't reach their ends.
Inputs may be any that keep to these rules, and one draw needn't show every extreme that they name: `doc_start`: one or two tokens after the first begin a new document. `expert_ids`: each token names 10 different experts; among the tokens of one device (aligned blocks of 512 // 32 rows) no expert is named more than 2 times, a bound that some block reaches.
All inputs are finite; a program needn't handle non-finite values.
Results may differ from the reference program's by a relative error of at most 0.014.
Values may be sent and summed in bfloat16 or wider, within the bound.
No kernel may reach another device: no remote copies, remote signals or barrier semaphores. Data moves between devices by JAX's collectives and lax.ppermute only.
A program may use at most 64 MiB of HBM per device.

```python
import math
import jax
import jax.numpy as jnp
import numpy as np
from jax import lax

D = 2048
HV = 32
DK = 128
DV = 128
FFE = 512
TOP = 10
TOK_DEV = 512
PROMPT_SPAN_LEN = 4096
EXPERTS = 256
MOST = 2
N_EXP = 32


def head_slow(key):
    share = 0.5
    return jax.random.uniform(jax.random.fold_in(key, 17), (HV,)) < share


def draw_log_decay(key, part):
    slow = head_slow(key)
    first_key = jax.random.fold_in(key, 31)
    second_key = jax.random.fold_in(key, 32)
    third_key = jax.random.fold_in(key, 33)
    fourth_key = jax.random.fold_in(key, 34)
    entry_factor = jnp.exp(jax.random.uniform(first_key, (HV, PROMPT_SPAN_LEN), minval=-0.6931, maxval=0.6931))
    groups = PROMPT_SPAN_LEN // TOK_DEV
    chip_factor = jnp.exp(jax.random.uniform(second_key, (HV, groups), minval=-0.6931, maxval=0.6931))
    chip_factor = jnp.repeat(chip_factor, TOK_DEV, axis=1)
    starting_shift = jnp.where(slow, 0.25 / PROMPT_SPAN_LEN, 0.025)
    chip_slots = jax.random.permutation(third_key, PROMPT_SPAN_LEN)[:3]
    span_index = jnp.sum((jnp.arange(PROMPT_SPAN_LEN)[None, :] == chip_slots[:, None]).astype(jnp.float32), axis=0)
    objective_value = jax.random.uniform(fourth_key, (HV,), minval=0.2, maxval=0.5)
    return -starting_shift[:, None] * entry_factor * chip_factor + jnp.log(1.0 - objective_value)[:, None] * span_index[None, :]


def draw_write_rate(key, part):
    slow = head_slow(key)
    unit = jax.random.uniform(jax.random.fold_in(key, 41), (HV, PROMPT_SPAN_LEN))
    lower = jnp.where(slow, jnp.log(0.001), jnp.log(0.1))
    return jnp.exp(lower[:, None] + jnp.log(10.0) * unit)


def draw_doc_start(key, part):
    chip_slots = jax.random.randint(jax.random.fold_in(key, 3), (2,), 1, PROMPT_SPAN_LEN)
    return jnp.zeros((PROMPT_SPAN_LEN,), jnp.int32).at[chip_slots].set(1)


def level_of(rng, dims, cuts, least, top_value):
    gain, own = 1.0, jax.random.fold_in(rng, 6)
    for dim, shards_of in cuts:
        heights = jnp.exp(jax.random.uniform(jax.random.fold_in(own, dim), (shards_of,), jnp.float32, least / len(cuts), top_value / len(cuts)))
        gain = gain * jnp.repeat(heights, dims[dim] // shards_of).reshape([-1 if axis == dim else 1 for axis in range(len(dims))])
    return gain


def assign_block(rng, own, number, rows, count, top, reach, slope):
    order = jax.random.permutation(rng, count)
    packed, common = shares(count, rows * top, reach, slope, True), shares(count, rows * top, reach, slope, False)
    places = jnp.arange(count)

    def named(sizes, turn):
        used = int((sizes > 0).sum())
        fixed = max(1, used // 4)
        passed = fixed + (places - fixed + turn * (used - fixed)) % max(1, count - fixed)
        return jnp.zeros((count,), jnp.int32).at[order[jnp.where(places < fixed, places, passed)]].set(jnp.asarray(sizes, jnp.int32))

    sizes = jnp.where(number % 4 == 0, named(packed, number // 4), named(common, number - number // 4 - 1))
    mixed = jax.random.permutation(jax.random.fold_in(own, 3), count)
    giver, taker = mixed[0:count // 2 * 2:2], mixed[1:count // 2 * 2:2]
    room = jnp.minimum(sizes[giver] - 1, reach - sizes[taker]) // 2
    room = jnp.where((giver == order[0]) | (taker == order[0]) | (sizes[taker] == 0), 0, jnp.maximum(room, 0))
    passed = jax.random.randint(jax.random.fold_in(own, 4), (count // 2,), 0, 1 << 20) % (room + 1)
    sizes = sizes.at[giver].add(-passed).at[taker].add(passed)
    items = jnp.searchsorted(jnp.cumsum(sizes), jnp.arange(rows * top), side="right").astype(jnp.int32)
    table = items.reshape(top, rows).T
    table = table[jax.random.permutation(jax.random.fold_in(own, 1), rows)]
    turn = jax.random.randint(jax.random.fold_in(own, 2), (rows, 1), 0, top)
    return jnp.take_along_axis(table, (jnp.arange(top)[None, :] + turn) % top, axis=1)


def shares(amount, total, most, skew, full):
    portions = [(1 << 20) // math.isqrt(grade ** skew) + 1 for grade in range(1, amount + 1)]
    largest = most if full else min(most, max(-(-total // amount), total * portions[0] // sum(portions)))
    least = 1 if total - largest >= amount - 1 else 0
    given, spare = [largest] + [least] * (amount - 1), total - largest - least * (amount - 1)
    while spare > 0:
        candidates = [i for i in range(1, amount) if given[i] < largest] or [i for i in range(1, amount) if given[i] < most]
        whole, budget = sum([portions[i] for i in candidates]), spare
        for i in candidates:
            addition = min(most - given[i], max(1, budget * portions[i] // whole), spare)
            given[i] = given[i] + addition
            spare = spare - addition
    return np.array(given)


def scatter_about(stream_key, extent, spread, bound, shards=(), held_as=jnp.bfloat16):
    loudness = level_of(stream_key, extent, shards, -0.22, 0.18) if shards else 1.0
    values = jax.random.normal(stream_key, extent, jnp.float32) * spread * loudness
    return jnp.minimum(jnp.maximum(values, -bound), bound).astype(held_as)


def setup_inputs(seed: int = 0) -> dict:
    streams_of = jax.random.split(jax.random.key(seed), 17)
    query_rows = scatter_about(streams_of[0], (PROMPT_SPAN_LEN, HV * DK), 1.0, 6.0, ((0, 8), (1, 32)))
    key_rows = scatter_about(streams_of[1], (PROMPT_SPAN_LEN, HV * DK), 1.0, 6.0, ((0, 8), (1, 32)))
    value_rows = scatter_about(streams_of[2], (PROMPT_SPAN_LEN, HV * DV), 1.0, 6.0, ((0, 8), (1, 32)))
    output_gate = scatter_about(streams_of[3], (PROMPT_SPAN_LEN, HV * DV), 1.0, 6.0, ((0, 8), (1, 32)))
    log_decay = draw_log_decay(jax.random.fold_in(streams_of[16], 71), 0)
    write_rate = draw_write_rate(jax.random.fold_in(streams_of[16], 71), 0)
    doc_start = draw_doc_start(jax.random.fold_in(streams_of[16], 71), 0)
    state_in = scatter_about(streams_of[7], (HV, DV, DK), 1.0, 6.0, ((0, 32),), jnp.float32)
    head_gain = jnp.clip(1.0 + 0.1 * jax.random.normal(streams_of[8], (DV,), jnp.float32), 0.5, 1.5)
    out_weight = scatter_about(streams_of[9], (HV * DV, D), (HV * DV) ** -0.5, 0.09375, ((0, 32),))
    residual = scatter_about(streams_of[10], (PROMPT_SPAN_LEN, D), 1.0, 6.0, ((0, 256),))
    post_gain = jnp.clip(1.0 + 0.1 * jax.random.normal(streams_of[11], (D,), jnp.float32), 0.5, 1.5)
    expert_ids_keys = jax.random.split(jax.random.fold_in(streams_of[12], 1), PROMPT_SPAN_LEN // (TOK_DEV // N_EXP))
    expert_ids_turns = jax.random.permutation(jax.random.fold_in(streams_of[12], 3), PROMPT_SPAN_LEN // (TOK_DEV // N_EXP))
    expert_ids = jax.vmap(lambda own, number: assign_block(jax.random.fold_in(streams_of[12], 2), own, number, TOK_DEV // N_EXP, EXPERTS, TOP, MOST, 2))(expert_ids_keys, expert_ids_turns).reshape((PROMPT_SPAN_LEN, TOP))
    expert_scale = jnp.clip(0.02 + 0.18 * jax.random.uniform(streams_of[13], (PROMPT_SPAN_LEN, TOP), jnp.float32) ** level_of(streams_of[13], (PROMPT_SPAN_LEN, TOP), ((0, 256),), -0.2, 0.2), 0.02, 0.2)
    w_gate_up = scatter_about(streams_of[14], (EXPERTS, D, 2 * FFE), D ** -0.5, 0.125, ((0, 256),))
    w_down = scatter_about(streams_of[15], (EXPERTS, FFE, D), FFE ** -0.5, 0.25, ((0, 256),))
    return {"query_rows": query_rows, "key_rows": key_rows, "value_rows": value_rows, "output_gate": output_gate, "log_decay": log_decay, "write_rate": write_rate, "doc_start": doc_start, "state_in": state_in, "head_gain": head_gain, "out_weight": out_weight, "residual": residual, "post_gain": post_gain, "expert_ids": expert_ids, "expert_scale": expert_scale, "w_gate_up": w_gate_up, "w_down": w_down}


def contract(form, left, right):
    return jnp.einsum(form, left, right, precision=lax.Precision.HIGHEST)

def reference(query_rows, key_rows, value_rows, output_gate, log_decay, write_rate, doc_start, state_in, head_gain, out_weight, residual, post_gain, expert_ids, expert_scale, w_gate_up, w_down):
    query = query_rows.astype(jnp.float32).reshape(PROMPT_SPAN_LEN, HV, DK)
    key = key_rows.astype(jnp.float32).reshape(PROMPT_SPAN_LEN, HV, DK)
    key = key * lax.rsqrt(lax.optimization_barrier(jnp.sum(key * key, axis=-1, keepdims=True)) + 1e-06)
    value = value_rows.astype(jnp.float32).reshape(PROMPT_SPAN_LEN, HV, DV)
    keep = jnp.exp(log_decay.T) * (1.0 - doc_start.astype(jnp.float32))[:, None]
    rate = write_rate.T

    def advance(state, inputs):
        query_now, key_now, value_now, keep_now, rate_now = inputs
        kept = keep_now[:, None, None] * state
        predicted = contract('hvk,hk->hv', kept, key_now)
        state = kept + contract('hv,hk->hvk', rate_now[:, None] * (value_now - predicted), key_now)
        return (state, contract('hvk,hk->hv', state, query_now))
    final, head_out = lax.scan(advance, state_in, (query, key, value, keep, rate))
    gate = output_gate.astype(jnp.float32).reshape(PROMPT_SPAN_LEN, HV, DV)
    scaled = head_out * lax.rsqrt(lax.optimization_barrier(jnp.mean(head_out * head_out, axis=-1, keepdims=True)) + 1e-06)
    gated = (scaled * head_gain * jax.nn.silu(gate)).astype(jnp.bfloat16).reshape(PROMPT_SPAN_LEN, HV * DV)
    attended = jnp.dot(gated, out_weight, preferred_element_type=jnp.float32)
    stream = (residual.astype(jnp.float32) + attended).astype(jnp.bfloat16)
    wide = stream.astype(jnp.float32)
    normed = (wide * lax.rsqrt(lax.optimization_barrier(jnp.mean(wide * wide, axis=-1, keepdims=True)) + 1e-06) * post_gain).astype(jnp.bfloat16)
    limit = EXPERTS * MOST

    def expert_pass(total, inputs):
        expert, gate_up, down = inputs
        matches = expert_ids == expert
        weight = lax.optimization_barrier(jnp.sum(jnp.where(matches, expert_scale, 0.0), axis=1))
        chosen = jnp.any(matches, axis=1)
        picked = jnp.nonzero(chosen, size=limit, fill_value=0)[0]
        count = jnp.sum(chosen.astype(jnp.int32))
        live = jnp.arange(limit) < count
        rows = normed[picked]
        both = jnp.dot(rows, gate_up, preferred_element_type=jnp.float32)
        hidden = (jax.nn.silu(both[:, :FFE]) * both[:, FFE:]).astype(jnp.bfloat16)
        result = jnp.dot(hidden, down, preferred_element_type=jnp.float32).astype(jnp.bfloat16)
        weight_rows = jnp.where(live, weight[picked], 0.0)
        total = total.at[picked].add(weight_rows[:, None] * result.astype(jnp.float32))
        return (total, None)
    moe, unused = lax.scan(expert_pass, jnp.zeros((PROMPT_SPAN_LEN, D), jnp.float32), (jnp.arange(EXPERTS, dtype=jnp.int32), w_gate_up, w_down))
    return (stream.astype(jnp.float32) + moe).astype(jnp.bfloat16)
```

```python
import functools

import jax
import jax.numpy as jnp
from jax import lax
from jax.experimental import pallas as pl
from jax.experimental.pallas import tpu as pltpu
from jax.sharding import Mesh, PartitionSpec as P

F32 = jnp.float32
BF = jnp.bfloat16
C = 128
NCH = 4
VM = pl.BlockSpec(memory_space=pltpu.VMEM)

NN = (((1,), (0,)), ((), ()))
NT = (((1,), (1,)), ((), ()))
TN = (((0,), (0,)), ((), ()))


def mm(a, b, dims=NN):
    return lax.dot_general(a, b, dims, preferred_element_type=F32)


def split(a):
    hi = a.astype(BF)
    lo = (a - hi.astype(F32)).astype(BF)
    return hi, lo


def d2(a, b, dims=NN):
    hi, lo = split(a)
    return mm(hi, b, dims) + mm(lo, b, dims)


def d3(a, b, dims=NN):
    ah, al = split(a)
    bh, bl = split(b)
    return mm(ah, bh, dims) + (mm(ah, bl, dims) + mm(al, bh, dims))


def iota2(shape, dim):
    return lax.broadcasted_iota(jnp.int32, shape, dim)


def call(body, outs, n_in, flops, scratch=(), vmem=None):
    single = not isinstance(outs, (tuple, list))
    bytes_accessed = 1 << 20
    return pl.pallas_call(
        body,
        out_shape=outs,
        in_specs=[VM] * n_in,
        out_specs=VM if single else tuple([VM] * len(outs)),
        scratch_shapes=list(scratch),
        compiler_params=pltpu.CompilerParams(vmem_limit_bytes=vmem or (12 << 20)),
        cost_estimate=pl.CostEstimate(
            flops=flops, bytes_accessed=bytes_accessed, transcendentals=0
        ),
    )


def prep_body(key, value, log_decay, rate, doc, e_out, u_out, dr_out, sc_out, prefix, own, sent):
    row = iota2((C, C), 0)
    col = iota2((C, C), 1)
    tri = (row <= col).astype(F32)
    eye = (row == col).astype(F32)
    span = [slice(c * C, (c + 1) * C) for c in range(NCH)]
    rows = jnp.concatenate(
        [log_decay[:, s] for s in span] + [doc[:, s].astype(F32) for s in span], axis=0
    )
    sums = lax.dot_general(
        rows, tri, NN, precision=lax.Precision.HIGHEST, preferred_element_type=F32
    )
    same8 = (row // 8) == (col // 8)
    systems, rates, starts, ends, lasts, rrows, keys = [], [], [], [], [], [], []
    for c in range(NCH):
        k = key[span[c], :]
        kf = k.astype(F32)
        norm = lax.rsqrt(jnp.sum(kf * kf, axis=1, keepdims=True) + 1e-6)
        rcol = jnp.broadcast_to(norm, (C, C))
        rrow = rcol.T
        lrow = jnp.broadcast_to(sums[c : c + 1, :], (C, C))
        zrow = jnp.broadcast_to(sums[NCH + c : NCH + c + 1, :], (C, C))
        brow = jnp.broadcast_to(rate[:, span[c]], (C, C))
        lcol = lrow.T
        zcol = zrow.T
        bcol = brow.T
        mask = (row >= col) & (zcol == zrow)
        decay = jnp.where(mask, jnp.exp(jnp.where(mask, lcol - lrow, 0.0)), 0.0)
        dr = decay * rrow
        inner = mm(k, k, NT)
        systems.append(jnp.where(row > col, bcol * rcol * dr * inner, 0.0))
        llast = lrow[:, C - 1 : C]
        zlast = zrow[:, C - 1 : C]
        starts.append(jnp.where(zrow == 0.0, jnp.exp(lrow), 0.0))
        ends.append(jnp.where(zrow == zlast, jnp.exp(llast - lrow), 0.0) * rrow)
        lasts.append(jnp.where(zlast == 0.0, jnp.exp(llast), 0.0))
        sc_out[span[c], :] = jnp.where(zcol == 0.0, jnp.exp(lcol), 0.0)
        dr_out[span[c], :] = dr
        rates.append(brow)
        rrows.append(rrow)
        keys.append(k)
    neg = [jnp.where(same8, -a, 0.0) for a in systems]
    sq = [d3(a, a) for a in neg]
    inv = [eye + a for a in neg]
    inv = [a + d3(a, b) for a, b in zip(inv, sq)]
    sq = [d3(a, a) for a in sq]
    inv = [a + d3(a, b) for a, b in zip(inv, sq)]
    size = 8
    while size < C:
        pair = ((row // (2 * size)) == (col // (2 * size))) & ((row // size) != (col // size))
        off = [jnp.where(pair, a, 0.0) for a in systems]
        half = [d3(a, b) for a, b in zip(off, inv)]
        inv = [a - d3(a, b) for a, b in zip(inv, half)]
        size *= 2
    update = [d2(x * b, value[span[c], :]) for c, (x, b) in enumerate(zip(inv, rates))]
    erase = [
        d2(x * (b * s * r), k) for x, b, s, r, k in zip(inv, rates, starts, rrows, keys)
    ]
    local = []
    for c in range(NCH):
        e_out[span[c], :] = erase[c]
        u_out[span[c], :] = update[c]
        both = jnp.concatenate([erase[c].T * ends[c], update[c].T * ends[c]], axis=0)
        moved = d2(both, keys[c])
        local.append((eye * lasts[c] - moved[:C, :], moved[C:, :]))
    total = jnp.concatenate([local[0][0], local[0][1]], axis=0)
    for c in range(1, NCH):
        prefix[c - 1] = total
        step = d3(total, local[c][0])
        total = jnp.concatenate([step[:C, :], step[C:, :] + local[c][1]], axis=0)
    own[...] = total
    sent[...] = total.astype(BF)


def pair_body(own, other, out):
    at = lax.axis_index("c") == 0
    mine = own[...]
    theirs = other[...].astype(F32)
    early = jnp.where(at, mine, theirs)
    late = jnp.where(at, theirs, mine)
    step = d3(early, late[:C, :])
    out[:C, :] = step[:C, :].astype(BF)
    out[C:, :] = (step[C:, :] + late[C:, :]).astype(BF)


def local_out_body(query, key, e_in, u_in, dr_in, sc_in, prefix, g_out, o_out):
    for c in range(NCH):
        s = slice(c * C, (c + 1) * C)
        q = query[s, :]
        scores = mm(q, key[s, :], NT) * dr_in[s, :]
        both = d3(scores, jnp.concatenate([e_in[s, :], u_in[s, :]], axis=1))
        lead = sc_in[s, :] * q.astype(F32) - both[:, :C]
        rest = both[:, C:]
        if c == 0:
            g_out[s, :] = lead
            o_out[s, :] = rest
        else:
            more = d3(lead, prefix[c - 1], NT)
            g_out[s, :] = more[:, :C]
            o_out[s, :] = rest + more[:, C:]


def gate_body(g_in, o_in, gate, gain, state_in, near, mid, far, other, o0, o1, o2, o3, buf):
    y = lax.axis_index("y")
    state = state_in[...]
    for k, ref in ((3, far), (2, mid), (1, near)):
        moved = d2(state, ref[:C, :]) + ref[C:, :].astype(F32)
        state = jnp.where(y >= k, moved, state)
    moved = d2(state, other[:C, :]) + other[C:, :].astype(F32)
    state = jnp.where(lax.axis_index("c") == 1, moved, state)
    head = d3(g_in[...], state, NT) + o_in[...]
    scaled = head * lax.rsqrt(jnp.mean(head * head, axis=1, keepdims=True) + 1e-6)
    x = gate[...].astype(F32)
    gated = scaled * gain[...] * (x / (1.0 + jnp.exp(-x)))
    buf[...] = gated.astype(BF).reshape(32, 16, C)
    me = lax.axis_index("x")
    for k, ref in enumerate((o0, o1, o2, o3)):
        to = lax.rem(me + k, 4)
        for z in range(8):
            ref[z * 16 : (z + 1) * 16, :] = buf[z * 4 + to]


def project_body(g0, g1, g2, g3, w0, w1, w2, w3, out):
    gs = [g[...] for g in (g0, g1, g2, g3)]
    for n in range(0, 2048, 512):
        total = mm(gs[0], w0[:, n : n + 512])
        for g, w in zip(gs[1:], (w1, w2, w3)):
            total = total + mm(g, w[:, n : n + 512])
        out[:, :, n : n + 512] = total.astype(BF).reshape(8, 16, 512)


def stream_body(parts, residual, gain, stream_out, normed_out):
    total = parts[0].astype(F32)
    for z in range(1, 8):
        total = total + parts[z].astype(F32)
    stream = (residual[...].astype(F32) + total).astype(BF)
    stream_out[...] = stream
    wide = stream.astype(F32)
    scale = lax.rsqrt(jnp.mean(wide * wide, axis=1, keepdims=True) + 1e-6)
    normed_out[...] = (wide * scale * gain[...]).astype(BF)


def route_body(m0, m1, m2, m3, pick_out, high_out, low_out):
    meta = jnp.concatenate([m0[...], m1[...], m2[...], m3[...]], axis=0)
    dest = iota2((64, 64), 1)
    token = iota2((64, 64), 0)
    expert = ((dest // 8) * 32 + lax.axis_index("zh") * 8 + dest % 8).astype(F32)
    chosen = jnp.zeros((64, 64), F32)
    scale = jnp.zeros((64, 64), F32)
    for k in range(10):
        hit = meta[:, k : k + 1] == expert
        chosen = jnp.where(hit, 1.0, chosen)
        scale = jnp.where(hit, meta[:, 10 + k : 11 + k], scale)
    before = (dest < token).astype(BF)
    rank = mm(before, chosen.astype(BF))
    place = jnp.where(chosen > 0.0, rank, -1.0).astype(BF)
    slot = iota2((64, 512), 1)
    spread = ((slot // 8) == iota2((64, 512), 0)).astype(BF)
    pick = mm(place, spread) == (slot % 8).astype(F32)
    high, low = split(scale)
    pick_out[...] = jnp.where(pick, 1.0, 0.0).astype(BF)
    high_out[...] = jnp.where(pick, mm(high, spread), 0.0).astype(BF)
    low_out[...] = jnp.where(pick, mm(low, spread), 0.0).astype(BF)


def dispatch_body(pick, n0, n1, n2, n3, out):
    rows = jnp.concatenate([n0[...], n1[...], n2[...], n3[...]], axis=0)
    choose = pick[...]
    for n in range(0, 2048, 512):
        out[:, n : n + 512] = mm(choose, rows[:, n : n + 512], TN).astype(BF)


def combine_body(high, low, rows, p0, p1, p2, p3):
    for n in range(0, 2048, 512):
        part = rows[:, n : n + 512]
        total = mm(high[...], part) + mm(low[...], part)
        p0[:, n : n + 512] = total[0:16]
        p1[:, n : n + 512] = total[16:32].astype(BF)
        p2[:, n : n + 512] = total[32:48].astype(BF)
        p3[:, n : n + 512] = total[48:64].astype(BF)


def final_body(stream, p0, p1, p2, p3, out):
    total = p0[...] + p1[...].astype(F32) + p2[...].astype(F32) + p3[...].astype(F32)
    out[...] = (stream[...].astype(F32) + total).astype(BF)


def shifted(array, axis, size, by):
    return lax.ppermute(array, axis, [(i, (i + by) % size) for i in range(size)])


def shape(dims, dtype):
    return jax.ShapeDtypeStruct(dims, dtype)


def local(
    query_rows,
    key_rows,
    value_rows,
    output_gate,
    log_decay,
    write_rate,
    doc_start,
    state_in,
    head_gain,
    out_weight,
    residual,
    post_gain,
    expert_ids,
    expert_scale,
    w_gate_up,
    w_down,
):
    weights = [out_weight] + [shifted(out_weight, "x", 4, k) for k in (1, 2, 3)]
    meta = jnp.concatenate([expert_ids.astype(F32), expert_scale], axis=1)
    metas = [meta] + [shifted(meta, "zh", 4, k) for k in (1, 2, 3)]

    big = shape((512, C), F32)
    erase, update, dr, start, prefix, own, sent = call(
        prep_body,
        (big, big, big, big, shape((3, 256, C), F32), shape((256, C), F32), shape((256, C), BF)),
        5,
        2_000_000_000,
    )(key_rows, value_rows, log_decay, write_rate, doc_start.reshape(1, 512))
    other = shifted(sent, "c", 2, 1)
    pick, high, low = call(
        route_body,
        (shape((64, 512), BF), shape((64, 512), BF), shape((64, 512), BF)),
        4,
        100_000_000,
    )(*metas)
    pair = call(pair_body, shape((256, C), BF), 2, 50_000_000)(own, other)
    near, mid, far = [
        lax.ppermute(pair, "y", [(i, i + k) for i in range(4 - k)]) for k in (1, 2, 3)
    ]
    lead, rest = call(local_out_body, (big, big), 7, 1_000_000_000)(
        query_rows, key_rows, erase, update, dr, start, prefix
    )
    slab = shape((128, C), BF)
    slabs = call(
        gate_body,
        (slab, slab, slab, slab),
        9,
        400_000_000,
        scratch=[pltpu.VMEM((32, 16, C), BF)],
    )(
        lead,
        rest,
        output_gate,
        head_gain.reshape(1, C),
        state_in.reshape(C, C),
        near,
        mid,
        far,
        other,
    )
    gated = [slabs[0]] + [shifted(slabs[k], "x", 4, k) for k in (1, 2, 3)]
    partial = call(project_body, shape((8, 16, 2048), BF), 8, 400_000_000)(*gated, *weights)
    parts = lax.all_to_all(partial, ("zh", "zl"), 0, 0, tiled=True)
    row_block = shape((16, 2048), BF)
    stream, normed = call(stream_body, (row_block, row_block), 3, 10_000_000)(
        parts, residual, post_gain.reshape(1, 2048)
    )
    gathered = [normed] + [shifted(normed, "zh", 4, k) for k in (1, 2, 3)]
    outgoing = call(dispatch_body, shape((512, 2048), BF), 5, 200_000_000)(pick, *gathered)
    axes = ("y", "c", "zl", "x")
    arrived = lax.all_to_all(outgoing.reshape(64, 8, 2048), axes, 0, 0, tiled=True)
    flat = arrived.reshape(512, 2048)
    both = jnp.dot(flat, w_gate_up[0], preferred_element_type=F32)
    hidden = (jax.nn.silu(both[:, :512]) * both[:, 512:]).astype(BF)
    result = jnp.dot(hidden, w_down[0], preferred_element_type=F32).astype(BF)
    returned = lax.all_to_all(result.reshape(64, 8, 2048), axes, 0, 0, tiled=True)
    p0, p1, p2, p3 = call(
        combine_body,
        (shape((16, 2048), F32), row_block, row_block, row_block),
        3,
        300_000_000,
    )(high, low, returned.reshape(512, 2048))
    back = [shifted(p, "zh", 4, -k) for k, p in ((1, p1), (2, p2), (3, p3))]
    return call(final_body, row_block, 5, 1_000_000)(stream, p0, *back)


def solution(mesh):
    torus = Mesh(mesh.devices.reshape(4, 2, 4, 2, 4), ("y", "c", "zh", "zl", "x"))
    seq = ("y", "c")
    exp = ("zh", "zl", "x")
    every = seq + exp
    return jax.shard_map(
        local,
        mesh=torus,
        in_specs=(
            P(seq, exp),
            P(seq, exp),
            P(seq, exp),
            P(seq, exp),
            P(exp, seq),
            P(exp, seq),
            P(seq),
            P(exp, None, None),
            P(),
            P(exp, None),
            P(every, None),
            P(),
            P(every, None),
            P(every, None),
            P(every, None, None),
            P(every, None, None),
        ),
        out_specs=P(every, None),
        check_vma=False,
    )
```

```python
import functools

import jax
import jax.numpy as jnp
from jax import lax
from jax.experimental import pallas as pl
from jax.experimental.pallas import tpu as pltpu
from jax.sharding import Mesh, PartitionSpec as P

F32 = jnp.float32
BF = jnp.bfloat16
C = 128
NCH = 4
VM = pl.BlockSpec(memory_space=pltpu.VMEM)

NN = (((1,), (0,)), ((), ()))
NT = (((1,), (1,)), ((), ()))
TN = (((0,), (0,)), ((), ()))


def mm(a, b, dims=NN):
    return lax.dot_general(a, b, dims, preferred_element_type=F32)


def split(a):
    hi = a.astype(BF)
    lo = (a - hi.astype(F32)).astype(BF)
    return hi, lo


def d2(a, b, dims=NN):
    hi, lo = split(a)
    return mm(hi, b, dims) + mm(lo, b, dims)


def d3(a, b, dims=NN):
    ah, al = split(a)
    bh, bl = split(b)
    return mm(ah, bh, dims) + (mm(ah, bl, dims) + mm(al, bh, dims))


def iota2(shape, dim):
    return lax.broadcasted_iota(jnp.int32, shape, dim)


def call(body, outs, n_in, flops, scratch=(), space=pltpu.VMEM):
    single = not isinstance(outs, (tuple, list))
    bytes_accessed = 1 << 20
    return pl.pallas_call(
        body,
        out_shape=outs,
        in_specs=[pl.BlockSpec(memory_space=space)] * n_in,
        out_specs=VM if single else tuple([VM] * len(outs)),
        scratch_shapes=list(scratch),
        compiler_params=pltpu.CompilerParams(vmem_limit_bytes=12 << 20),
        cost_estimate=pl.CostEstimate(
            flops=flops, bytes_accessed=bytes_accessed, transcendentals=0
        ),
    )


def prep_body(*refs):
    sources, outs, held, sems = refs[:5], refs[5:12], refs[12:17], refs[17]
    copies = [
        pltpu.make_async_copy(a, b, sems.at[i]) for i, (a, b) in enumerate(zip(sources, held))
    ]
    for copy in copies:
        copy.start()
    for copy in copies:
        copy.wait()
    key, value, log_decay, rate, doc = held
    e_out, u_out, dr_out, sc_out, prefix, own, sent = outs
    row = iota2((C, C), 0)
    col = iota2((C, C), 1)
    tri = (row <= col).astype(F32)
    eye = (row == col).astype(F32)
    span = [slice(c * C, (c + 1) * C) for c in range(NCH)]
    rows = jnp.concatenate(
        [log_decay[:, s] for s in span] + [doc[:, s].astype(F32) for s in span], axis=0
    )
    sums = lax.dot_general(
        rows, tri, NN, precision=lax.Precision.HIGHEST, preferred_element_type=F32
    )
    same8 = (row // 8) == (col // 8)
    systems, rates, starts, ends, lasts, rrows, keys = [], [], [], [], [], [], []
    for c in range(NCH):
        k = key[span[c], :]
        kf = k.astype(F32)
        norm = lax.rsqrt(jnp.sum(kf * kf, axis=1, keepdims=True) + 1e-6)
        rcol = jnp.broadcast_to(norm, (C, C))
        rrow = rcol.T
        lrow = jnp.broadcast_to(sums[c : c + 1, :], (C, C))
        zrow = jnp.broadcast_to(sums[NCH + c : NCH + c + 1, :], (C, C))
        brow = jnp.broadcast_to(rate[:, span[c]], (C, C))
        lcol = lrow.T
        zcol = zrow.T
        bcol = brow.T
        mask = (row >= col) & (zcol == zrow)
        decay = jnp.where(mask, jnp.exp(jnp.where(mask, lcol - lrow, 0.0)), 0.0)
        dr = decay * rrow
        inner = mm(k, k, NT)
        systems.append(jnp.where(row > col, bcol * rcol * dr * inner, 0.0))
        llast = lrow[:, C - 1 : C]
        zlast = zrow[:, C - 1 : C]
        starts.append(jnp.where(zrow == 0.0, jnp.exp(lrow), 0.0))
        ends.append(jnp.where(zrow == zlast, jnp.exp(llast - lrow), 0.0) * rrow)
        lasts.append(jnp.where(zlast == 0.0, jnp.exp(llast), 0.0))
        sc_out[span[c], :] = jnp.where(zcol == 0.0, jnp.exp(lcol), 0.0)
        dr_out[span[c], :] = dr
        rates.append(brow)
        rrows.append(rrow)
        keys.append(k)
    neg = [jnp.where(same8, -a, 0.0) for a in systems]
    sq = [d3(a, a) for a in neg]
    inv = [eye + a for a in neg]
    inv = [a + d3(a, b) for a, b in zip(inv, sq)]
    sq = [d3(a, a) for a in sq]
    inv = [a + d3(a, b) for a, b in zip(inv, sq)]
    size = 8
    while size < C:
        pair = ((row // (2 * size)) == (col // (2 * size))) & ((row // size) != (col // size))
        off = [jnp.where(pair, a, 0.0) for a in systems]
        half = [d3(a, b) for a, b in zip(off, inv)]
        inv = [a - d3(a, b) for a, b in zip(inv, half)]
        size *= 2
    update = [d2(x * b, value[span[c], :]) for c, (x, b) in enumerate(zip(inv, rates))]
    erase = [
        d2(x * (b * s * r), k) for x, b, s, r, k in zip(inv, rates, starts, rrows, keys)
    ]
    local = []
    for c in range(NCH):
        e_out[span[c], :] = erase[c]
        u_out[span[c], :] = update[c]
        both = jnp.concatenate([erase[c].T * ends[c], update[c].T * ends[c]], axis=0)
        moved = d2(both, keys[c])
        local.append((eye * lasts[c] - moved[:C, :], moved[C:, :]))
    total = jnp.concatenate([local[0][0], local[0][1]], axis=0)
    for c in range(1, NCH):
        prefix[c - 1] = total
        step = d3(total, local[c][0])
        total = jnp.concatenate([step[:C, :], step[C:, :] + local[c][1]], axis=0)
    own[...] = total
    sent[...] = total.astype(BF)


def pair_body(own, other, out):
    at = lax.axis_index("c") == 0
    mine = own[...]
    theirs = other[...].astype(F32)
    early = jnp.where(at, mine, theirs)
    late = jnp.where(at, theirs, mine)
    step = d3(early, late[:C, :])
    out[:C, :] = step[:C, :].astype(BF)
    out[C:, :] = (step[C:, :] + late[C:, :]).astype(BF)


def local_out_body(query, key, e_in, u_in, dr_in, sc_in, prefix, g_out, o_out):
    for c in range(NCH):
        s = slice(c * C, (c + 1) * C)
        q = query[s, :]
        scores = mm(q, key[s, :], NT) * dr_in[s, :]
        both = d3(scores, jnp.concatenate([e_in[s, :], u_in[s, :]], axis=1))
        lead = sc_in[s, :] * q.astype(F32) - both[:, :C]
        rest = both[:, C:]
        if c == 0:
            g_out[s, :] = lead
            o_out[s, :] = rest
        else:
            more = d3(lead, prefix[c - 1], NT)
            g_out[s, :] = more[:, :C]
            o_out[s, :] = rest + more[:, C:]


def gate_body(g_in, o_in, gate, gain, state_in, near, mid, far, other, o0, o1, o2, o3, buf):
    y = lax.axis_index("y")
    state = state_in[...]
    for k, ref in ((3, far), (2, mid), (1, near)):
        moved = d2(state, ref[:C, :]) + ref[C:, :].astype(F32)
        state = jnp.where(y >= k, moved, state)
    moved = d2(state, other[:C, :]) + other[C:, :].astype(F32)
    state = jnp.where(lax.axis_index("c") == 1, moved, state)
    head = d3(g_in[...], state, NT) + o_in[...]
    scaled = head * lax.rsqrt(jnp.mean(head * head, axis=1, keepdims=True) + 1e-6)
    x = gate[...].astype(F32)
    gated = scaled * gain[...] * (x / (1.0 + jnp.exp(-x)))
    buf[...] = gated.astype(BF).reshape(32, 16, C)
    me = lax.axis_index("x")
    for k, ref in enumerate((o0, o1, o2, o3)):
        to = lax.rem(me + k, 4)
        for z in range(8):
            ref[z * 16 : (z + 1) * 16, :] = buf[z * 4 + to]


def project_body(g0, g1, g2, g3, w0, w1, w2, w3, out):
    gs = [g[...] for g in (g0, g1, g2, g3)]
    for n in range(0, 2048, 512):
        total = mm(gs[0], w0[:, n : n + 512])
        for g, w in zip(gs[1:], (w1, w2, w3)):
            total = total + mm(g, w[:, n : n + 512])
        out[:, :, n : n + 512] = total.astype(BF).reshape(8, 16, 512)


def stream_body(parts, residual, gain, stream_out, normed_out):
    total = parts[0].astype(F32)
    for z in range(1, 8):
        total = total + parts[z].astype(F32)
    stream = (residual[...].astype(F32) + total).astype(BF)
    stream_out[...] = stream
    wide = stream.astype(F32)
    scale = lax.rsqrt(jnp.mean(wide * wide, axis=1, keepdims=True) + 1e-6)
    normed_out[...] = (wide * scale * gain[...]).astype(BF)


def route_body(m0, m1, m2, m3, pick_out, high_out, low_out):
    meta = jnp.concatenate([m0[...], m1[...], m2[...], m3[...]], axis=0)
    dest = iota2((64, 64), 1)
    token = iota2((64, 64), 0)
    expert = ((dest // 8) * 32 + lax.axis_index("zh") * 8 + dest % 8).astype(F32)
    chosen = jnp.zeros((64, 64), F32)
    scale = jnp.zeros((64, 64), F32)
    for k in range(10):
        hit = meta[:, k : k + 1] == expert
        chosen = jnp.where(hit, 1.0, chosen)
        scale = jnp.where(hit, meta[:, 10 + k : 11 + k], scale)
    before = (dest < token).astype(BF)
    rank = mm(before, chosen.astype(BF))
    place = jnp.where(chosen > 0.0, rank, -1.0).astype(BF)
    slot = iota2((64, 512), 1)
    spread = ((slot // 8) == iota2((64, 512), 0)).astype(BF)
    pick = mm(place, spread) == (slot % 8).astype(F32)
    high, low = split(scale)
    pick_out[...] = jnp.where(pick, 1.0, 0.0).astype(BF)
    high_out[...] = jnp.where(pick, mm(high, spread), 0.0).astype(BF)
    low_out[...] = jnp.where(pick, mm(low, spread), 0.0).astype(BF)


def dispatch_body(pick, n0, n1, n2, n3, out):
    rows = jnp.concatenate([n0[...], n1[...], n2[...], n3[...]], axis=0)
    choose = pick[...]
    for n in range(0, 2048, 512):
        out[:, n : n + 512] = mm(choose, rows[:, n : n + 512], TN).astype(BF)


def combine_body(high, low, rows, p0, p1, p2, p3):
    for n in range(0, 2048, 512):
        part = rows[:, n : n + 512]
        total = mm(high[...], part) + mm(low[...], part)
        p0[:, n : n + 512] = total[0:16]
        p1[:, n : n + 512] = total[16:32].astype(BF)
        p2[:, n : n + 512] = total[32:48].astype(BF)
        p3[:, n : n + 512] = total[48:64].astype(BF)


def final_body(stream, p0, p1, p2, p3, out):
    total = p0[...] + p1[...].astype(F32) + p2[...].astype(F32) + p3[...].astype(F32)
    out[...] = (stream[...].astype(F32) + total).astype(BF)


def shifted(array, axis, size, by):
    return lax.ppermute(array, axis, [(i, (i + by) % size) for i in range(size)])


def shape(dims, dtype):
    return jax.ShapeDtypeStruct(dims, dtype)


def local(
    query_rows,
    key_rows,
    value_rows,
    output_gate,
    log_decay,
    write_rate,
    doc_start,
    state_in,
    head_gain,
    out_weight,
    residual,
    post_gain,
    expert_ids,
    expert_scale,
    w_gate_up,
    w_down,
):
    weights = [out_weight] + [shifted(out_weight, "x", 4, k) for k in (1, 2, 3)]
    meta = jnp.concatenate([expert_ids.astype(F32), expert_scale], axis=1)

    big = shape((512, C), F32)
    erase, update, dr, start, prefix, own, sent = call(
        prep_body,
        (big, big, big, big, shape((3, 256, C), F32), shape((256, C), F32), shape((256, C), BF)),
        5,
        2_000_000_000,
        scratch=[
            pltpu.VMEM((512, C), BF),
            pltpu.VMEM((512, C), BF),
            pltpu.VMEM((1, 512), F32),
            pltpu.VMEM((1, 512), F32),
            pltpu.VMEM((1, 512), jnp.int32),
            pltpu.SemaphoreType.DMA((5,)),
        ],
        space=pltpu.HBM,
    )(
        *[
            pltpu.with_memory_space_constraint(a, pltpu.HBM)
            for a in (key_rows, value_rows, log_decay, write_rate, doc_start.reshape(1, 512))
        ]
    )
    other = shifted(sent, "c", 2, 1)
    pair = call(pair_body, shape((256, C), BF), 2, 50_000_000)(own, other)
    near, mid, far = [
        lax.ppermute(pair, "y", [(i, i + k) for i in range(4 - k)]) for k in (1, 2, 3)
    ]
    lead, rest = call(local_out_body, (big, big), 7, 1_000_000_000)(
        query_rows, key_rows, erase, update, dr, start, prefix
    )
    slab = shape((128, C), BF)
    slabs = call(
        gate_body,
        (slab, slab, slab, slab),
        9,
        400_000_000,
        scratch=[pltpu.VMEM((32, 16, C), BF)],
    )(
        lead,
        rest,
        output_gate,
        head_gain.reshape(1, C),
        state_in.reshape(C, C),
        near,
        mid,
        far,
        other,
    )
    gated = [slabs[0]] + [shifted(slabs[k], "x", 4, k) for k in (1, 2, 3)]
    partial = call(project_body, shape((8, 16, 2048), BF), 8, 400_000_000)(*gated, *weights)
    partial, meta = lax.optimization_barrier((partial, meta))
    parts = lax.all_to_all(partial, ("zh", "zl"), 0, 0, tiled=True)
    metas = [meta] + [shifted(meta, "zh", 4, k) for k in (2, 1, 3)]
    pick, high, low = call(
        route_body,
        (shape((64, 512), BF), shape((64, 512), BF), shape((64, 512), BF)),
        4,
        100_000_000,
    )(*metas)
    parts, pick, high, low = lax.optimization_barrier((parts, pick, high, low))
    row_block = shape((16, 2048), BF)
    stream, normed = call(stream_body, (row_block, row_block), 3, 10_000_000)(
        parts, residual, post_gain.reshape(1, 2048)
    )
    gathered = [normed] + [shifted(normed, "zh", 4, k) for k in (2, 1, 3)]
    outgoing = call(dispatch_body, shape((512, 2048), BF), 5, 200_000_000)(pick, *gathered)
    axes = ("y", "c", "zl", "x")
    arrived = lax.all_to_all(outgoing.reshape(64, 8, 2048), axes, 0, 0, tiled=True)
    flat = arrived.reshape(512, 2048)
    both = jnp.dot(flat, w_gate_up[0], preferred_element_type=F32)
    hidden = (jax.nn.silu(both[:, :512]) * both[:, 512:]).astype(BF)
    result = jnp.dot(hidden, w_down[0], preferred_element_type=F32).astype(BF)
    returned = lax.all_to_all(result.reshape(64, 8, 2048), axes, 0, 0, tiled=True)
    p0, p1, p2, p3 = call(
        combine_body,
        (shape((16, 2048), F32), row_block, row_block, row_block),
        3,
        300_000_000,
    )(high, low, returned.reshape(512, 2048))
    back = [shifted(p, "zh", 4, -k) for k, p in ((2, p1), (1, p2), (3, p3))]
    return call(final_body, row_block, 5, 1_000_000)(stream, p0, *back)


def solution(mesh):
    torus = Mesh(mesh.devices.reshape(4, 2, 4, 2, 4), ("y", "c", "zh", "zl", "x"))
    seq = ("y", "c")
    exp = ("zh", "zl", "x")
    every = seq + exp
    return jax.shard_map(
        local,
        mesh=torus,
        in_specs=(
            P(seq, exp),
            P(seq, exp),
            P(seq, exp),
            P(seq, exp),
            P(exp, seq),
            P(exp, seq),
            P(seq),
            P(exp, None, None),
            P(),
            P(exp, None),
            P(every, None),
            P(),
            P(every, None),
            P(every, None),
            P(every, None, None),
            P(every, None, None),
        ),
        out_specs=P(every, None),
        check_vma=False,
    )
```

```python
import functools

import jax
import jax.numpy as jnp
from jax import lax
from jax.experimental import pallas as pl
from jax.experimental.pallas import tpu as pltpu
from jax.sharding import Mesh, PartitionSpec as P

F32 = jnp.float32
BF = jnp.bfloat16
C = 128
NCH = 4
VM = pl.BlockSpec(memory_space=pltpu.VMEM)

NN = (((1,), (0,)), ((), ()))
NT = (((1,), (1,)), ((), ()))
TN = (((0,), (0,)), ((), ()))


def mm(a, b, dims=NN):
    return lax.dot_general(a, b, dims, preferred_element_type=F32)


def split(a):
    hi = a.astype(BF)
    lo = (a - hi.astype(F32)).astype(BF)
    return hi, lo


def d2(a, b, dims=NN):
    hi, lo = split(a)
    return mm(hi, b, dims) + mm(lo, b, dims)


def d3(a, b, dims=NN):
    ah, al = split(a)
    bh, bl = split(b)
    return mm(ah, bh, dims) + (mm(ah, bl, dims) + mm(al, bh, dims))


def iota2(shape, dim):
    return lax.broadcasted_iota(jnp.int32, shape, dim)


def call(body, outs, n_in, flops, scratch=(), space=pltpu.VMEM):
    single = not isinstance(outs, (tuple, list))
    bytes_accessed = 1 << 20
    return pl.pallas_call(
        body,
        out_shape=outs,
        in_specs=[pl.BlockSpec(memory_space=space)] * n_in,
        out_specs=VM if single else tuple([VM] * len(outs)),
        scratch_shapes=list(scratch),
        compiler_params=pltpu.CompilerParams(vmem_limit_bytes=12 << 20),
        cost_estimate=pl.CostEstimate(
            flops=flops, bytes_accessed=bytes_accessed, transcendentals=0
        ),
    )


def prep_body(*refs):
    sources, outs, held, sems = refs[:7], refs[7:14], refs[14:21], refs[21]
    copies = [
        pltpu.make_async_copy(a, b, sems.at[i]) for i, (a, b) in enumerate(zip(sources, held))
    ]
    for copy in copies:
        copy.start()
    for copy in copies:
        copy.wait()
    key, value, log_decay, rate, doc, ids, scale = held
    e_out, u_out, dr_out, sc_out, prefix, own, sent = outs
    row = iota2((C, C), 0)
    col = iota2((C, C), 1)
    tri = (row <= col).astype(F32)
    eye = (row == col).astype(F32)
    span = [slice(c * C, (c + 1) * C) for c in range(NCH)]
    rows = jnp.concatenate(
        [log_decay[:, s] for s in span] + [doc[:, s].astype(F32) for s in span], axis=0
    )
    sums = lax.dot_general(
        rows, tri, NN, precision=lax.Precision.HIGHEST, preferred_element_type=F32
    )
    same8 = (row // 8) == (col // 8)
    systems, rates, starts, ends, lasts, rrows, keys = [], [], [], [], [], [], []
    for c in range(NCH):
        k = key[span[c], :]
        kf = k.astype(F32)
        norm = lax.rsqrt(jnp.sum(kf * kf, axis=1, keepdims=True) + 1e-6)
        rcol = jnp.broadcast_to(norm, (C, C))
        rrow = rcol.T
        lrow = jnp.broadcast_to(sums[c : c + 1, :], (C, C))
        zrow = jnp.broadcast_to(sums[NCH + c : NCH + c + 1, :], (C, C))
        brow = jnp.broadcast_to(rate[:, span[c]], (C, C))
        lcol = lrow.T
        zcol = zrow.T
        bcol = brow.T
        mask = (row >= col) & (zcol == zrow)
        decay = jnp.where(mask, jnp.exp(jnp.where(mask, lcol - lrow, 0.0)), 0.0)
        dr = decay * rrow
        inner = mm(k, k, NT)
        systems.append(jnp.where(row > col, bcol * rcol * dr * inner, 0.0))
        llast = lrow[:, C - 1 : C]
        zlast = zrow[:, C - 1 : C]
        starts.append(jnp.where(zrow == 0.0, jnp.exp(lrow), 0.0))
        ends.append(jnp.where(zrow == zlast, jnp.exp(llast - lrow), 0.0) * rrow)
        lasts.append(jnp.where(zlast == 0.0, jnp.exp(llast), 0.0))
        sc_out[span[c], :] = jnp.where(zcol == 0.0, jnp.exp(lcol), 0.0)
        dr_out[span[c], :] = dr
        rates.append(brow)
        rrows.append(rrow)
        keys.append(k)
    neg = [jnp.where(same8, -a, 0.0) for a in systems]
    sq = [d3(a, a) for a in neg]
    inv = [eye + a for a in neg]
    inv = [a + d3(a, b) for a, b in zip(inv, sq)]
    sq = [d3(a, a) for a in sq]
    inv = [a + d3(a, b) for a, b in zip(inv, sq)]
    for size in (8, 32):
        group = (row // (4 * size)) == (col // (4 * size))
        off = [jnp.where(group & ((row // size) != (col // size)), a, 0.0) for a in systems]
        step = [d3(a, b) for a, b in zip(inv, off)]
        twice = [d3(a, a) for a in step]
        inv = [a - d3(b, a) for a, b in zip(inv, step)]
        inv = [a + d3(b, a) for a, b in zip(inv, twice)]
    update = [d2(x * b, value[span[c], :]) for c, (x, b) in enumerate(zip(inv, rates))]
    erase = [
        d2(x * (b * s * r), k) for x, b, s, r, k in zip(inv, rates, starts, rrows, keys)
    ]
    local = []
    for c in range(NCH):
        e_out[span[c], :] = erase[c]
        u_out[span[c], :] = update[c]
        both = jnp.concatenate([erase[c].T * ends[c], update[c].T * ends[c]], axis=0)
        moved = d2(both, keys[c])
        local.append((eye * lasts[c] - moved[:C, :], moved[C:, :]))
    stacked = [jnp.concatenate(pair, axis=0) for pair in local]

    def follow(early, late):
        step = d3(early, late[:C, :])
        return jnp.concatenate([step[:C, :], step[C:, :] + late[C:, :]], axis=0)

    second = follow(stacked[0], stacked[1])
    tail = follow(stacked[2], stacked[3])
    total = follow(second, tail)
    prefix[0] = stacked[0]
    prefix[1] = second
    prefix[2] = follow(second, stacked[2])
    own[...] = total
    sent[: 2 * C, :] = total.astype(BF)
    high, mid = split(scale[...])
    low = (scale[...] - high.astype(F32) - mid.astype(F32)).astype(BF)
    meta = jnp.zeros((16, C), F32)
    for n, part in enumerate((ids[...].astype(F32).astype(BF), high, mid, low)):
        move = iota2((10, C), 1) == iota2((10, C), 0) + 10 * n
        meta = meta + mm(part, move.astype(BF))
    sent[2 * C :, :] = meta.astype(BF)


def pair_body(own, other, out):
    at = lax.axis_index("c") == 0
    mine = own[...]
    theirs = other[: 2 * C, :].astype(F32)
    early = jnp.where(at, mine, theirs)
    late = jnp.where(at, theirs, mine)
    step = d3(early, late[:C, :])
    out[:C, :] = step[:C, :].astype(BF)
    out[C:, :] = (step[C:, :] + late[C:, :]).astype(BF)


def local_out_body(query, key, e_in, u_in, dr_in, sc_in, prefix, g_out, o_out):
    for c in range(NCH):
        s = slice(c * C, (c + 1) * C)
        q = query[s, :]
        scores = mm(q, key[s, :], NT) * dr_in[s, :]
        both = d3(scores, jnp.concatenate([e_in[s, :], u_in[s, :]], axis=1))
        lead = sc_in[s, :] * q.astype(F32) - both[:, :C]
        rest = both[:, C:]
        if c == 0:
            g_out[s, :] = lead
            o_out[s, :] = rest
        else:
            more = d3(lead, prefix[c - 1], NT)
            g_out[s, :] = more[:, :C]
            o_out[s, :] = rest + more[:, C:]


def gate_body(g_in, o_in, gate, gain, state_in, near, mid, far, other, o0, o1, o2, o3, buf):
    y = lax.axis_index("y")
    state = state_in[...]
    for k, ref in ((3, far), (2, mid), (1, near)):
        moved = d2(state, ref[:C, :]) + ref[C:, :].astype(F32)
        state = jnp.where(y >= k, moved, state)
    moved = d2(state, other[:C, :]) + other[C : 2 * C, :].astype(F32)
    state = jnp.where(lax.axis_index("c") == 1, moved, state)
    head = d3(g_in[...], state, NT) + o_in[...]
    scaled = head * lax.rsqrt(jnp.mean(head * head, axis=1, keepdims=True) + 1e-6)
    x = gate[...].astype(F32)
    gated = scaled * gain[...] * (x / (1.0 + jnp.exp(-x)))
    buf[...] = gated.astype(BF).reshape(32, 16, C)
    me = lax.axis_index("x")
    for k, ref in enumerate((o0, o1, o2, o3)):
        to = lax.rem(me + k, 4)
        for z in range(8):
            ref[z * 16 : (z + 1) * 16, :] = buf[z * 4 + to]


def project_body(g0, g1, g2, g3, w0, w1, w2, w3, sent, other, out):
    gs = [g[...] for g in (g0, g1, g2, g3)]
    move = (iota2((C, C), 1) == iota2((C, C), 0) + 64).astype(BF)
    meta = sent[2 * C :, :].astype(F32) + mm(other[2 * C :, :], move)
    out[:, :, 2048:] = jnp.broadcast_to(meta.astype(BF)[None], (8, 16, C))
    for n in range(0, 2048, 512):
        total = mm(gs[0], w0[:, n : n + 512])
        for g, w in zip(gs[1:], (w1, w2, w3)):
            total = total + mm(g, w[:, n : n + 512])
        out[:, :, n : n + 512] = total.astype(BF).reshape(8, 16, 512)


def stream_body(parts, residual, gain, stream_out, normed_out):
    total = parts[0, :, :2048].astype(F32)
    for z in range(1, 8):
        total = total + parts[z, :, :2048].astype(F32)
    stream = (residual[...].astype(F32) + total).astype(BF)
    stream_out[...] = stream
    wide = stream.astype(F32)
    scale = lax.rsqrt(jnp.mean(wide * wide, axis=1, keepdims=True) + 1e-6)
    normed_out[...] = (wide * scale * gain[...]).astype(BF)


def route_body(parts, pick_out, high_out, low_out):
    zh = lax.axis_index("zh")
    zl = lax.axis_index("zl")
    at = lax.axis_index("c")
    move = (iota2((C, C), 0) == iota2((C, C), 1) + 64).astype(BF)

    def block(back):
        mine = parts[lax.rem(zh - back + 4, 4) * 2 + zl, :, 2048:]
        return mine.astype(F32), mm(mine, move)

    near, far = block(1 + 2 * at), block(3 - 2 * at)
    meta = jnp.concatenate([*block(0), *block(2), *near, far[1], far[0]], axis=0)
    dest = iota2((128, 32), 1)
    expert = (((dest // 8) * 2 + at) * 32 + zh * 8 + dest % 8).astype(F32)
    chosen = jnp.zeros((128, 32), F32)
    scale = jnp.zeros((128, 32), F32)
    for k in range(10):
        hit = meta[:, k : k + 1] == expert
        chosen = jnp.where(hit, 1.0, chosen)
        value = (
            meta[:, 10 + k : 11 + k] + meta[:, 20 + k : 21 + k] + meta[:, 30 + k : 31 + k]
        )
        scale = jnp.where(hit, value, scale)
    before = (iota2((128, 128), 1) < iota2((128, 128), 0)).astype(BF)
    rank = mm(before, chosen.astype(BF))
    place = jnp.where(chosen > 0.0, rank, -1.0).astype(BF)
    slot = iota2((32, 512), 1)
    spread = ((slot // 16) == iota2((32, 512), 0)).astype(BF)
    pick = mm(place, spread) == (iota2((128, 512), 1) % 16).astype(F32)
    high, low = split(scale)
    pick_out[...] = jnp.where(pick, 1.0, 0.0).astype(BF)
    high_out[...] = jnp.where(pick, mm(high, spread), 0.0).astype(BF)
    low_out[...] = jnp.where(pick, mm(low, spread), 0.0).astype(BF)


def dispatch_body(pick, own, partner, two, two_partner, one, one_partner, out):
    parts = (own, partner, two, two_partner, one, one_partner)
    rows = jnp.concatenate([p[...] for p in parts], axis=0)
    choose = pick[...]
    for n in range(0, 2048, 512):
        out[:, n : n + 512] = mm(choose, rows[:, n : n + 512], TN).astype(BF)


def combine_body(high, low, rows, own, two, one, give):
    for n in range(0, 2048, 512):
        part = rows[:, n : n + 512]
        total = mm(high[...], part) + mm(low[...], part)
        own[:, n : n + 512] = total[0:16]
        two[:, n : n + 512] = total[32:48]
        one[:, n : n + 512] = total[64:96]
        give[0:16, n : n + 512] = total[16:32].astype(BF)
        give[16:32, n : n + 512] = total[48:64].astype(BF)
        give[32:64, n : n + 512] = total[96:128].astype(BF)


def join_body(own, two, one, got, own_out, two_out, one_out):
    own_out[...] = own[...] + got[0:16, :].astype(F32)
    two_out[...] = (two[...] + got[16:32, :].astype(F32)).astype(BF)
    one_out[...] = (one[...] + got[32:64, :].astype(F32)).astype(BF)


def final_body(stream, own, two, one, partner, out):
    total = own[...] + two[...].astype(F32) + one[0:16, :].astype(F32) + partner[...].astype(F32)
    out[...] = (stream[...].astype(F32) + total).astype(BF)


def by_core(array, sign):
    pairs = [(z, (z + sign) % 4) for z in range(4)]
    pairs += [(4 + z, 4 + (z - sign) % 4) for z in range(4)]
    return lax.ppermute(array, ("c", "zh"), pairs)


def shifted(array, axis, size, by):
    return lax.ppermute(array, axis, [(i, (i + by) % size) for i in range(size)])


def shape(dims, dtype):
    return jax.ShapeDtypeStruct(dims, dtype)


def local(
    query_rows,
    key_rows,
    value_rows,
    output_gate,
    log_decay,
    write_rate,
    doc_start,
    state_in,
    head_gain,
    out_weight,
    residual,
    post_gain,
    expert_ids,
    expert_scale,
    w_gate_up,
    w_down,
):
    weights = [out_weight] + [shifted(out_weight, "x", 4, k) for k in (1, 2, 3)]

    big = shape((512, C), F32)
    erase, update, dr, start, prefix, own, sent = call(
        prep_body,
        (big, big, big, big, shape((3, 256, C), F32), shape((256, C), F32), shape((272, C), BF)),
        7,
        2_000_000_000,
        scratch=[
            pltpu.VMEM((512, C), BF),
            pltpu.VMEM((512, C), BF),
            pltpu.VMEM((1, 512), F32),
            pltpu.VMEM((1, 512), F32),
            pltpu.VMEM((1, 512), jnp.int32),
            pltpu.VMEM((16, 10), jnp.int32),
            pltpu.VMEM((16, 10), F32),
            pltpu.SemaphoreType.DMA((7,)),
        ],
        space=pltpu.HBM,
    )(
        *[
            pltpu.with_memory_space_constraint(a, pltpu.HBM)
            for a in (
                key_rows,
                value_rows,
                log_decay,
                write_rate,
                doc_start.reshape(1, 512),
                expert_ids,
                expert_scale,
            )
        ]
    )
    other = shifted(sent, "c", 2, 1)
    pair = call(pair_body, shape((256, C), BF), 2, 50_000_000)(own, other)
    near, mid, far = [
        lax.ppermute(pair, "y", [(i, i + k) for i in range(4 - k)]) for k in (1, 2, 3)
    ]
    lead, rest = call(local_out_body, (big, big), 7, 1_000_000_000)(
        query_rows, key_rows, erase, update, dr, start, prefix
    )
    slab = shape((128, C), BF)
    slabs = call(
        gate_body,
        (slab, slab, slab, slab),
        9,
        400_000_000,
        scratch=[pltpu.VMEM((32, 16, C), BF)],
    )(
        lead,
        rest,
        output_gate,
        head_gain.reshape(1, C),
        state_in.reshape(C, C),
        near,
        mid,
        far,
        other,
    )
    gated = [slabs[0]] + [shifted(slabs[k], "x", 4, k) for k in (1, 2, 3)]
    partial = call(project_body, shape((8, 16, 2048 + C), BF), 10, 400_000_000)(
        *gated, *weights, sent, other
    )
    parts = lax.all_to_all(partial, ("zh", "zl"), 0, 0, tiled=True)
    row_block = shape((16, 2048), BF)
    stream, normed = call(stream_body, (row_block, row_block), 3, 10_000_000)(
        parts, residual, post_gain.reshape(1, 2048)
    )
    partner = shifted(normed, "c", 2, 1)
    two = shifted(normed, "zh", 4, 2)
    one = by_core(jnp.concatenate([normed, partner], axis=0), 1)
    two_partner = shifted(two, "c", 2, 1)
    one_partner = shifted(one, "c", 2, 1)
    table = shape((128, 512), BF)
    pick, high, low = call(route_body, (table, table, table), 1, 100_000_000)(parts)
    outgoing = call(dispatch_body, shape((512, 2048), BF), 7, 200_000_000)(
        pick, normed, partner, two, two_partner, one, one_partner
    )
    axes = ("y", "zl", "x")
    arrived = lax.all_to_all(outgoing.reshape(32, 16, 2048), axes, 0, 0, tiled=True)
    flat = arrived.reshape(512, 2048)
    both = jnp.dot(flat, w_gate_up[0], preferred_element_type=F32)
    hidden = (jax.nn.silu(both[:, :512]) * both[:, 512:]).astype(BF)
    result = jnp.dot(hidden, w_down[0], preferred_element_type=F32).astype(BF)
    returned = lax.all_to_all(result.reshape(32, 16, 2048), axes, 0, 0, tiled=True)
    wide_block = shape((16, 2048), F32)
    own, two, one, give = call(
        combine_body,
        (wide_block, wide_block, shape((32, 2048), F32), shape((64, 2048), BF)),
        3,
        300_000_000,
    )(high, low, returned.reshape(512, 2048))
    got = shifted(give, "c", 2, 1)
    own, two, one = call(
        join_body, (wide_block, row_block, shape((32, 2048), BF)), 4, 1_000_000
    )(own, two, one, got)
    two = shifted(two, "zh", 4, 2)
    one = by_core(one, -1)
    last = shifted(one[16:], "c", 2, 1)
    return call(final_body, row_block, 5, 1_000_000)(stream, own, two, one, last)


def solution(mesh):
    torus = Mesh(mesh.devices.reshape(4, 2, 4, 2, 4), ("y", "c", "zh", "zl", "x"))
    seq = ("y", "c")
    exp = ("zh", "zl", "x")
    every = seq + exp
    return jax.shard_map(
        local,
        mesh=torus,
        in_specs=(
            P(seq, exp),
            P(seq, exp),
            P(seq, exp),
            P(seq, exp),
            P(exp, seq),
            P(exp, seq),
            P(seq),
            P(exp, None, None),
            P(),
            P(exp, None),
            P(every, None),
            P(),
            P(every, None),
            P(every, None),
            P(every, None, None),
            P(every, None, None),
        ),
        out_specs=P(every, None),
        check_vma=False,
    )
```

```python
import functools

import jax
import jax.numpy as jnp
from jax import lax
from jax.experimental import pallas as pl
from jax.experimental.pallas import tpu as pltpu
from jax.sharding import Mesh, PartitionSpec as P

F32 = jnp.float32
BF = jnp.bfloat16
C = 128
NCH = 4
ORDER = (2, 1, 3)
VM = pl.BlockSpec(memory_space=pltpu.VMEM)

NN = (((1,), (0,)), ((), ()))
NT = (((1,), (1,)), ((), ()))
TN = (((0,), (0,)), ((), ()))


def mm(a, b, dims=NN):
    return lax.dot_general(a, b, dims, preferred_element_type=F32)


def split(a):
    hi = a.astype(BF)
    lo = (a - hi.astype(F32)).astype(BF)
    return hi, lo


def d2(a, b, dims=NN):
    hi, lo = split(a)
    return mm(hi, b, dims) + mm(lo, b, dims)


def d3(a, b, dims=NN):
    ah, al = split(a)
    bh, bl = split(b)
    return mm(ah, bh, dims) + (mm(ah, bl, dims) + mm(al, bh, dims))


def iota2(shape, dim):
    return lax.broadcasted_iota(jnp.int32, shape, dim)


def call(body, outs, n_in, flops, scratch=(), space=pltpu.VMEM):
    single = not isinstance(outs, (tuple, list))
    bytes_accessed = 1 << 20
    return pl.pallas_call(
        body,
        out_shape=outs,
        in_specs=[pl.BlockSpec(memory_space=space)] * n_in,
        out_specs=VM if single else tuple([VM] * len(outs)),
        scratch_shapes=list(scratch),
        compiler_params=pltpu.CompilerParams(vmem_limit_bytes=12 << 20),
        cost_estimate=pl.CostEstimate(
            flops=flops, bytes_accessed=bytes_accessed, transcendentals=0
        ),
    )


def prep_body(*refs):
    sources, outs, held, sems = refs[:5], refs[5:12], refs[12:17], refs[17]
    copies = [
        pltpu.make_async_copy(a, b, sems.at[i]) for i, (a, b) in enumerate(zip(sources, held))
    ]
    for copy in copies:
        copy.start()
    for i in (2, 3, 4, 0):
        copies[i].wait()
    key, value, log_decay, rate, doc = held
    e_out, u_out, dr_out, sc_out, prefix, own, sent = outs
    row = iota2((C, C), 0)
    col = iota2((C, C), 1)
    tri = (row <= col).astype(F32)
    eye = (row == col).astype(F32)
    span = [slice(c * C, (c + 1) * C) for c in range(NCH)]
    rows = jnp.concatenate(
        [log_decay[:, s] for s in span] + [doc[:, s].astype(F32) for s in span], axis=0
    )
    sums = lax.dot_general(
        rows, tri, NN, precision=lax.Precision.HIGHEST, preferred_element_type=F32
    )
    same8 = (row // 8) == (col // 8)
    systems, rates, starts, ends, lasts, rrows, keys = [], [], [], [], [], [], []
    for c in range(NCH):
        k = key[span[c], :]
        kf = k.astype(F32)
        norm = lax.rsqrt(jnp.sum(kf * kf, axis=1, keepdims=True) + 1e-6)
        rcol = jnp.broadcast_to(norm, (C, C))
        rrow = rcol.T
        lrow = jnp.broadcast_to(sums[c : c + 1, :], (C, C))
        zrow = jnp.broadcast_to(sums[NCH + c : NCH + c + 1, :], (C, C))
        brow = jnp.broadcast_to(rate[:, span[c]], (C, C))
        lcol = lrow.T
        zcol = zrow.T
        bcol = brow.T
        mask = (row >= col) & (zcol == zrow)
        decay = jnp.where(mask, jnp.exp(jnp.where(mask, lcol - lrow, 0.0)), 0.0)
        dr = decay * rrow
        inner = mm(k, k, NT)
        systems.append(jnp.where(row > col, bcol * rcol * dr * inner, 0.0))
        llast = lrow[:, C - 1 : C]
        zlast = zrow[:, C - 1 : C]
        starts.append(jnp.where(zrow == 0.0, jnp.exp(lrow), 0.0))
        ends.append(jnp.where(zrow == zlast, jnp.exp(llast - lrow), 0.0) * rrow)
        lasts.append(jnp.where(zlast == 0.0, jnp.exp(llast), 0.0))
        sc_out[span[c], :] = jnp.where(zcol == 0.0, jnp.exp(lcol), 0.0)
        dr_out[span[c], :] = dr
        rates.append(brow)
        rrows.append(rrow)
        keys.append(k)
    neg = [jnp.where(same8, -a, 0.0) for a in systems]
    sq = [d3(a, a) for a in neg]
    inv = [eye + a for a in neg]
    inv = [a + d3(a, b) for a, b in zip(inv, sq)]
    sq = [d3(a, a) for a in sq]
    inv = [a + d3(a, b) for a, b in zip(inv, sq)]
    for size in (8, 32):
        group = (row // (4 * size)) == (col // (4 * size))
        off = [jnp.where(group & ((row // size) != (col // size)), a, 0.0) for a in systems]
        step = [d3(a, b) for a, b in zip(inv, off)]
        twice = [d3(a, a) for a in step]
        inv = [a - d3(b, a) for a, b in zip(inv, step)]
        inv = [a + d3(b, a) for a, b in zip(inv, twice)]
    copies[1].wait()
    update = [d2(x * b, value[span[c], :]) for c, (x, b) in enumerate(zip(inv, rates))]
    erase = [
        d2(x * (b * s * r), k) for x, b, s, r, k in zip(inv, rates, starts, rrows, keys)
    ]
    local = []
    for c in range(NCH):
        e_out[span[c], :] = erase[c]
        u_out[span[c], :] = update[c]
        both = jnp.concatenate([erase[c].T * ends[c], update[c].T * ends[c]], axis=0)
        moved = d2(both, keys[c])
        local.append((eye * lasts[c] - moved[:C, :], moved[C:, :]))
    stacked = [jnp.concatenate(pair, axis=0) for pair in local]

    def follow(early, late):
        step = d3(early, late[:C, :])
        return jnp.concatenate([step[:C, :], step[C:, :] + late[C:, :]], axis=0)

    second = follow(stacked[0], stacked[1])
    tail = follow(stacked[2], stacked[3])
    total = follow(second, tail)
    prefix[0] = stacked[0]
    prefix[1] = second
    prefix[2] = follow(second, stacked[2])
    own[...] = total
    sent[...] = total.astype(BF)


def pair_body(own, other, out):
    at = lax.axis_index("c") == 0
    mine = own[...]
    theirs = other[...].astype(F32)
    early = jnp.where(at, mine, theirs)
    late = jnp.where(at, theirs, mine)
    step = d3(early, late[:C, :])
    out[:C, :] = step[:C, :].astype(BF)
    out[C:, :] = (step[C:, :] + late[C:, :]).astype(BF)


def local_out_body(query, key, e_in, u_in, dr_in, sc_in, prefix, g_out, o_out):
    for c in range(NCH):
        s = slice(c * C, (c + 1) * C)
        q = query[s, :]
        scores = mm(q, key[s, :], NT) * dr_in[s, :]
        both = d3(scores, jnp.concatenate([e_in[s, :], u_in[s, :]], axis=1))
        lead = sc_in[s, :] * q.astype(F32) - both[:, :C]
        rest = both[:, C:]
        if c == 0:
            g_out[s, :] = lead
            o_out[s, :] = rest
        else:
            more = d3(lead, prefix[c - 1], NT)
            g_out[s, :] = more[:, :C]
            o_out[s, :] = rest + more[:, C:]


def gate_body(g_in, o_in, gate, gain, state_in, near, mid, far, other, o0, o1, o2, o3, buf):
    y = lax.axis_index("y")
    state = state_in[...]
    for k, ref in ((3, far), (2, mid), (1, near)):
        moved = d2(state, ref[:C, :]) + ref[C:, :].astype(F32)
        state = jnp.where(y >= k, moved, state)
    moved = d2(state, other[:C, :]) + other[C:, :].astype(F32)
    state = jnp.where(lax.axis_index("c") == 1, moved, state)
    head = d3(g_in[...], state, NT) + o_in[...]
    scaled = head * lax.rsqrt(jnp.mean(head * head, axis=1, keepdims=True) + 1e-6)
    x = gate[...].astype(F32)
    gated = scaled * gain[...] * (x / (1.0 + jnp.exp(-x)))
    buf[...] = gated.astype(BF).reshape(32, 16, C)
    me = lax.axis_index("x")
    for k, ref in enumerate((o0, o1, o2, o3)):
        to = lax.rem(me + k, 4)
        for z in range(8):
            ref[z * 16 : (z + 1) * 16, :] = buf[z * 4 + to]


def project_body(g0, g1, g2, g3, w0, w1, w2, w3, ids, scale, out):
    gs = [g[...] for g in (g0, g1, g2, g3)]
    high, rest = split(scale[...])
    mid = rest
    low = (scale[...] - high.astype(F32) - mid.astype(F32)).astype(BF)
    meta = jnp.zeros((16, C), F32)
    for n, part in enumerate((ids[...].astype(F32).astype(BF), high, mid, low)):
        move = iota2((10, C), 1) == iota2((10, C), 0) + 10 * n
        meta = meta + mm(part, move.astype(BF))
    out[:, :, 2048:] = jnp.broadcast_to(meta.astype(BF)[None], (8, 16, C))
    for n in range(0, 2048, 512):
        total = mm(gs[0], w0[:, n : n + 512])
        for g, w in zip(gs[1:], (w1, w2, w3)):
            total = total + mm(g, w[:, n : n + 512])
        out[:, :, n : n + 512] = total.astype(BF).reshape(8, 16, 512)


def stream_body(parts, residual, gain, stream_out, normed_out):
    total = parts[0, :, :2048].astype(F32)
    for z in range(1, 8):
        total = total + parts[z, :, :2048].astype(F32)
    stream = (residual[...].astype(F32) + total).astype(BF)
    stream_out[...] = stream
    wide = stream.astype(F32)
    scale = lax.rsqrt(jnp.mean(wide * wide, axis=1, keepdims=True) + 1e-6)
    normed_out[...] = (wide * scale * gain[...]).astype(BF)


def route_body(parts, pick_out, scale_out):
    zh = lax.axis_index("zh")
    zl = lax.axis_index("zl")
    meta = jnp.concatenate(
        [parts[lax.rem(zh - k + 4, 4) * 2 + zl, :, 2048:] for k in (0,) + ORDER], axis=0
    ).astype(F32)
    dest = iota2((64, 64), 1)
    token = iota2((64, 64), 0)
    expert = ((dest // 8) * 32 + zh * 8 + dest % 8).astype(F32)
    chosen = jnp.zeros((64, 64), F32)
    scale = jnp.zeros((64, 64), F32)
    for k in range(10):
        hit = meta[:, k : k + 1] == expert
        chosen = jnp.where(hit, 1.0, chosen)
        value = (
            meta[:, 10 + k : 11 + k] + meta[:, 20 + k : 21 + k] + meta[:, 30 + k : 31 + k]
        )
        scale = jnp.where(hit, value, scale)
    before = (dest < token).astype(BF)
    rank = mm(before, chosen.astype(BF))
    place = jnp.where(chosen > 0.0, rank, -1.0).astype(BF)
    slot = iota2((64, 512), 1)
    spread = ((slot // 8) == iota2((64, 512), 0)).astype(BF)
    pick = mm(place, spread) == (slot % 8).astype(F32)
    tall = iota2((512, 64), 0)
    spread_tall = ((tall // 8) == iota2((512, 64), 1)).astype(BF)
    pick_tall = mm(spread_tall, place, NT) == (tall % 8).astype(F32)
    high, low = split(scale)
    pick_out[...] = jnp.where(pick_tall, 1.0, 0.0).astype(BF)
    scale_out[0:64, :] = jnp.where(pick, mm(high, spread), 0.0).astype(BF)
    scale_out[64:128, :] = jnp.where(pick, mm(low, spread), 0.0).astype(BF)


def dispatch_body(pick, n0, n1, n2, n3, out):
    rows = jnp.concatenate([n0[...], n1[...], n2[...], n3[...]], axis=0)
    choose = pick[...]
    for n in range(0, 2048, 512):
        out[:, n : n + 512] = mm(choose, rows[:, n : n + 512]).astype(BF)


def combine_body(scale, rows, p0, p1, p2, p3):
    for n in range(0, 2048, 512):
        part = rows[:, n : n + 512]
        total = mm(scale[...], part)
        total = total[:64, :] + total[64:, :]
        p0[:, n : n + 512] = total[0:16]
        p1[:, n : n + 512] = total[16:32].astype(BF)
        p2[:, n : n + 512] = total[32:48].astype(BF)
        p3[:, n : n + 512] = total[48:64].astype(BF)


def final_body(stream, p0, p1, p2, p3, out):
    total = p0[...] + p1[...].astype(F32) + p2[...].astype(F32) + p3[...].astype(F32)
    out[...] = (stream[...].astype(F32) + total).astype(BF)


def shifted(array, axis, size, by):
    return lax.ppermute(array, axis, [(i, (i + by) % size) for i in range(size)])


def shape(dims, dtype):
    return jax.ShapeDtypeStruct(dims, dtype)


def local(
    query_rows,
    key_rows,
    value_rows,
    output_gate,
    log_decay,
    write_rate,
    doc_start,
    state_in,
    head_gain,
    out_weight,
    residual,
    post_gain,
    expert_ids,
    expert_scale,
    w_gate_up,
    w_down,
):
    weights = [out_weight] + [shifted(out_weight, "x", 4, k) for k in (1, 2, 3)]

    big = shape((512, C), F32)
    erase, update, dr, start, prefix, own, sent = call(
        prep_body,
        (big, big, big, big, shape((3, 256, C), F32), shape((256, C), F32), shape((256, C), BF)),
        5,
        2_000_000_000,
        scratch=[
            pltpu.VMEM((512, C), BF),
            pltpu.VMEM((512, C), BF),
            pltpu.VMEM((1, 512), F32),
            pltpu.VMEM((1, 512), F32),
            pltpu.VMEM((1, 512), jnp.int32),
            pltpu.SemaphoreType.DMA((5,)),
        ],
        space=pltpu.HBM,
    )(
        *[
            pltpu.with_memory_space_constraint(a, pltpu.HBM)
            for a in (key_rows, value_rows, log_decay, write_rate, doc_start.reshape(1, 512))
        ]
    )
    other = shifted(sent, "c", 2, 1)
    pair = call(pair_body, shape((256, C), BF), 2, 50_000_000)(own, other)
    near, mid, far = [
        lax.ppermute(pair, "y", [(i, i + k) for i in range(4 - k)]) for k in (1, 2, 3)
    ]
    lead, rest = call(local_out_body, (big, big), 7, 1_000_000_000)(
        query_rows, key_rows, erase, update, dr, start, prefix
    )
    slab = shape((128, C), BF)
    slabs = call(
        gate_body,
        (slab, slab, slab, slab),
        9,
        400_000_000,
        scratch=[pltpu.VMEM((32, 16, C), BF)],
    )(
        lead,
        rest,
        output_gate,
        head_gain.reshape(1, C),
        state_in.reshape(C, C),
        near,
        mid,
        far,
        other,
    )
    gated = [slabs[0]] + [shifted(slabs[k], "x", 4, k) for k in (1, 2, 3)]
    partial = call(project_body, shape((8, 16, 2048 + C), BF), 10, 400_000_000)(
        *gated, *weights, expert_ids, expert_scale
    )
    parts = lax.all_to_all(partial, ("zh", "zl"), 0, 0, tiled=True)
    row_block = shape((16, 2048), BF)
    stream, normed = call(stream_body, (row_block, row_block), 3, 10_000_000)(
        parts, residual, post_gain.reshape(1, 2048)
    )
    gathered = [normed] + [shifted(normed, "zh", 4, k) for k in ORDER]
    pick, scales = call(
        route_body,
        (shape((512, 64), BF), shape((128, 512), BF)),
        1,
        100_000_000,
    )(parts)
    outgoing = call(dispatch_body, shape((512, 2048), BF), 5, 200_000_000)(pick, *gathered)
    axes = ("y", "c", "zl", "x")
    arrived = lax.all_to_all(outgoing.reshape(64, 8, 2048), axes, 0, 0, tiled=True)
    flat = arrived.reshape(512, 2048)
    both = jnp.dot(flat, w_gate_up[0], preferred_element_type=F32)
    hidden = (jax.nn.silu(both[:, :512]) * both[:, 512:]).astype(BF)
    result = jnp.dot(hidden, w_down[0], preferred_element_type=F32).astype(BF)
    returned = lax.all_to_all(result.reshape(64, 8, 2048), axes, 0, 0, tiled=True)
    p0, p1, p2, p3 = call(
        combine_body,
        (shape((16, 2048), F32), row_block, row_block, row_block),
        2,
        300_000_000,
    )(scales, returned.reshape(512, 2048))
    back = [shifted(p, "zh", 4, -k) for k, p in zip(ORDER, (p1, p2, p3))]
    return call(final_body, row_block, 5, 1_000_000)(stream, p0, *back)


def solution(mesh):
    torus = Mesh(mesh.devices.reshape(4, 2, 4, 2, 4), ("y", "c", "zh", "zl", "x"))
    seq = ("y", "c")
    exp = ("zh", "zl", "x")
    every = seq + exp
    return jax.shard_map(
        local,
        mesh=torus,
        in_specs=(
            P(seq, exp),
            P(seq, exp),
            P(seq, exp),
            P(seq, exp),
            P(exp, seq),
            P(exp, seq),
            P(seq),
            P(exp, None, None),
            P(),
            P(exp, None),
            P(every, None),
            P(),
            P(every, None),
            P(every, None),
            P(every, None, None),
            P(every, None, None),
        ),
        out_specs=P(every, None),
        check_vma=False,
    )
```

```python
import functools

import jax
import jax.numpy as jnp
from jax import lax
from jax.experimental import pallas as pl
from jax.experimental.pallas import tpu as pltpu
from jax.sharding import Mesh, PartitionSpec as P

F32 = jnp.float32
BF = jnp.bfloat16
C = 128
NCH = 4
ORDER = (2, 1, 3)
VM = pl.BlockSpec(memory_space=pltpu.VMEM)

NN = (((1,), (0,)), ((), ()))
NT = (((1,), (1,)), ((), ()))
TN = (((0,), (0,)), ((), ()))


def mm(a, b, dims=NN):
    return lax.dot_general(a, b, dims, preferred_element_type=F32)


def split(a):
    hi = a.astype(BF)
    lo = (a - hi.astype(F32)).astype(BF)
    return hi, lo


def d2(a, b, dims=NN):
    hi, lo = split(a)
    return mm(hi, b, dims) + mm(lo, b, dims)


def d3(a, b, dims=NN):
    ah, al = split(a)
    bh, bl = split(b)
    return mm(ah, bh, dims) + (mm(ah, bl, dims) + mm(al, bh, dims))


def iota2(shape, dim):
    return lax.broadcasted_iota(jnp.int32, shape, dim)


def call(body, outs, n_in, flops, scratch=(), space=pltpu.VMEM):
    single = not isinstance(outs, (tuple, list))
    bytes_accessed = 1 << 20
    return pl.pallas_call(
        body,
        out_shape=outs,
        in_specs=[pl.BlockSpec(memory_space=space)] * n_in,
        out_specs=VM if single else tuple([VM] * len(outs)),
        scratch_shapes=list(scratch),
        compiler_params=pltpu.CompilerParams(vmem_limit_bytes=12 << 20),
        cost_estimate=pl.CostEstimate(
            flops=flops, bytes_accessed=bytes_accessed, transcendentals=0
        ),
    )


def prep_body(*refs):
    sources, outs, held, sems = refs[:5], refs[5:12], refs[12:17], refs[17]
    copies = [
        pltpu.make_async_copy(a, b, sems.at[i]) for i, (a, b) in enumerate(zip(sources, held))
    ]
    for copy in copies:
        copy.start()
    for i in (2, 3, 4, 0):
        copies[i].wait()
    key, value, log_decay, rate, doc = held
    e_out, u_out, dr_out, sc_out, prefix, own, sent = outs
    row = iota2((C, C), 0)
    col = iota2((C, C), 1)
    tri = (row <= col).astype(F32)
    eye = (row == col).astype(F32)
    span = [slice(c * C, (c + 1) * C) for c in range(NCH)]
    rows = jnp.concatenate(
        [log_decay[:, s] for s in span] + [doc[:, s].astype(F32) for s in span], axis=0
    )
    sums = lax.dot_general(
        rows, tri, NN, precision=lax.Precision.HIGHEST, preferred_element_type=F32
    )
    same8 = (row // 8) == (col // 8)
    systems, rates, starts, ends, lasts, rrows, keys = [], [], [], [], [], [], []
    for c in range(NCH):
        k = key[span[c], :]
        kf = k.astype(F32)
        norm = lax.rsqrt(jnp.sum(kf * kf, axis=1, keepdims=True) + 1e-6)
        rcol = jnp.broadcast_to(norm, (C, C))
        rrow = rcol.T
        lrow = jnp.broadcast_to(sums[c : c + 1, :], (C, C))
        zrow = jnp.broadcast_to(sums[NCH + c : NCH + c + 1, :], (C, C))
        brow = jnp.broadcast_to(rate[:, span[c]], (C, C))
        lcol = lrow.T
        zcol = zrow.T
        bcol = brow.T
        mask = (row >= col) & (zcol == zrow)
        decay = jnp.where(mask, jnp.exp(jnp.where(mask, lcol - lrow, 0.0)), 0.0)
        dr = decay * rrow
        inner = mm(k, k, NT)
        systems.append(jnp.where(row > col, bcol * rcol * dr * inner, 0.0))
        llast = lrow[:, C - 1 : C]
        zlast = zrow[:, C - 1 : C]
        starts.append(jnp.where(zrow == 0.0, jnp.exp(lrow), 0.0))
        ends.append(jnp.where(zrow == zlast, jnp.exp(llast - lrow), 0.0) * rrow)
        lasts.append(jnp.where(zlast == 0.0, jnp.exp(llast), 0.0))
        sc_out[span[c], :] = jnp.where(zcol == 0.0, jnp.exp(lcol), 0.0)
        dr_out[span[c], :] = dr
        rates.append(brow)
        rrows.append(rrow)
        keys.append(k)
    neg = [jnp.where(same8, -a, 0.0) for a in systems]
    sq = [d3(a, a) for a in neg]
    inv = [eye + a for a in neg]
    inv = [a + d3(a, b) for a, b in zip(inv, sq)]
    sq = [d3(a, a) for a in sq]
    inv = [a + d3(a, b) for a, b in zip(inv, sq)]
    for size in (8, 32):
        group = (row // (4 * size)) == (col // (4 * size))
        off = [jnp.where(group & ((row // size) != (col // size)), a, 0.0) for a in systems]
        step = [d3(a, b) for a, b in zip(inv, off)]
        twice = [d3(a, a) for a in step]
        inv = [a - d3(b, a) for a, b in zip(inv, step)]
        inv = [a + d3(b, a) for a, b in zip(inv, twice)]
    copies[1].wait()
    update = [d2(x * b, value[span[c], :]) for c, (x, b) in enumerate(zip(inv, rates))]
    erase = [
        d2(x * (b * s * r), k) for x, b, s, r, k in zip(inv, rates, starts, rrows, keys)
    ]
    local = []
    for c in range(NCH):
        e_out[span[c], :] = erase[c]
        u_out[span[c], :] = update[c]
        both = jnp.concatenate([erase[c].T * ends[c], update[c].T * ends[c]], axis=0)
        moved = d2(both, keys[c])
        local.append((eye * lasts[c] - moved[:C, :], moved[C:, :]))
    stacked = [jnp.concatenate(pair, axis=0) for pair in local]

    def follow(early, late):
        step = d3(early, late[:C, :])
        return jnp.concatenate([step[:C, :], step[C:, :] + late[C:, :]], axis=0)

    second = follow(stacked[0], stacked[1])
    tail = follow(stacked[2], stacked[3])
    total = follow(second, tail)
    prefix[0] = stacked[0]
    prefix[1] = second
    prefix[2] = follow(second, stacked[2])
    own[...] = total
    sent[...] = total.astype(BF)


def pair_body(own, other, out):
    at = lax.axis_index("c") == 0
    mine = own[...]
    theirs = other[...].astype(F32)
    early = jnp.where(at, mine, theirs)
    late = jnp.where(at, theirs, mine)
    step = d3(early, late[:C, :])
    out[:C, :] = step[:C, :].astype(BF)
    out[C:, :] = (step[C:, :] + late[C:, :]).astype(BF)


def local_out_body(query, key, e_in, u_in, dr_in, sc_in, prefix, g_out, o_out):
    for c in range(NCH):
        s = slice(c * C, (c + 1) * C)
        q = query[s, :]
        scores = mm(q, key[s, :], NT) * dr_in[s, :]
        both = d3(scores, jnp.concatenate([e_in[s, :], u_in[s, :]], axis=1))
        lead = sc_in[s, :] * q.astype(F32) - both[:, :C]
        rest = both[:, C:]
        if c == 0:
            g_out[s, :] = lead
            o_out[s, :] = rest
        else:
            more = d3(lead, prefix[c - 1], NT)
            g_out[s, :] = more[:, :C]
            o_out[s, :] = rest + more[:, C:]


def gate_body(g_in, o_in, gate, gain, state_in, near, mid, far, other, o0, o1, o2, o3, buf):
    y = lax.axis_index("y")
    state = state_in[...]
    for k, ref in ((3, far), (2, mid), (1, near)):
        moved = d2(state, ref[:C, :]) + ref[C:, :].astype(F32)
        state = jnp.where(y >= k, moved, state)
    moved = d2(state, other[:C, :]) + other[C:, :].astype(F32)
    state = jnp.where(lax.axis_index("c") == 1, moved, state)
    head = d3(g_in[...], state, NT) + o_in[...]
    scaled = head * lax.rsqrt(jnp.mean(head * head, axis=1, keepdims=True) + 1e-6)
    x = gate[...].astype(F32)
    gated = scaled * gain[...] * (x / (1.0 + jnp.exp(-x)))
    buf[...] = gated.astype(BF).reshape(32, 16, C)
    me = lax.axis_index("x")
    for k, ref in enumerate((o0, o1, o2, o3)):
        to = lax.rem(me + k, 4)
        for z in range(8):
            ref[z * 16 : (z + 1) * 16, :] = buf[z * 4 + to]


def project_body(g0, g1, g2, g3, w0, w1, w2, w3, ids, scale, out):
    gs = [g[...] for g in (g0, g1, g2, g3)]
    high, rest = split(scale[...])
    mid = rest
    low = (scale[...] - high.astype(F32) - mid.astype(F32)).astype(BF)
    meta = jnp.zeros((16, C), F32)
    for n, part in enumerate((ids[...].astype(F32).astype(BF), high, mid, low)):
        move = iota2((10, C), 1) == iota2((10, C), 0) + 10 * n
        meta = meta + mm(part, move.astype(BF))
    out[:, :, 2048:] = jnp.broadcast_to(meta.astype(BF)[None], (8, 16, C))
    for n in range(0, 2048, 512):
        total = mm(gs[0], w0[:, n : n + 512])
        for g, w in zip(gs[1:], (w1, w2, w3)):
            total = total + mm(g, w[:, n : n + 512])
        out[:, :, n : n + 512] = total.astype(BF).reshape(8, 16, 512)


def stream_body(parts, residual, gain, stream_out, normed_out):
    total = parts[0, :, :2048].astype(F32)
    for z in range(1, 8):
        total = total + parts[z, :, :2048].astype(F32)
    stream = (residual[...].astype(F32) + total).astype(BF)
    stream_out[...] = stream
    wide = stream.astype(F32)
    scale = lax.rsqrt(jnp.mean(wide * wide, axis=1, keepdims=True) + 1e-6)
    normed_out[...] = (wide * scale * gain[...]).astype(BF)


def route_body(parts, pick_out, scale_out):
    zh = lax.axis_index("zh")
    zl = lax.axis_index("zl")
    meta = jnp.concatenate(
        [parts[lax.rem(zh - k + 4, 4) * 2 + zl, :, 2048:] for k in (0,) + ORDER], axis=0
    ).astype(F32)
    dest = iota2((64, 64), 1)
    token = iota2((64, 64), 0)
    expert = ((dest // 8) * 32 + zh * 8 + dest % 8).astype(F32)
    chosen = jnp.zeros((64, 64), F32)
    scale = jnp.zeros((64, 64), F32)
    for k in range(10):
        hit = meta[:, k : k + 1] == expert
        chosen = jnp.where(hit, 1.0, chosen)
        value = (
            meta[:, 10 + k : 11 + k] + meta[:, 20 + k : 21 + k] + meta[:, 30 + k : 31 + k]
        )
        scale = jnp.where(hit, value, scale)
    before = (dest < token).astype(BF)
    rank = mm(before, chosen.astype(BF))
    place = jnp.where(chosen > 0.0, rank, -1.0).astype(BF)
    slot = iota2((64, 512), 1)
    spread = ((slot // 8) == iota2((64, 512), 0)).astype(BF)
    pick = mm(place, spread) == (slot % 8).astype(F32)
    tall = iota2((512, 64), 0)
    spread_tall = ((tall // 8) == iota2((512, 64), 1)).astype(BF)
    pick_tall = mm(spread_tall, place, NT) == (tall % 8).astype(F32)
    high, low = split(scale)
    pick_out[...] = jnp.where(pick_tall, 1.0, 0.0).astype(BF)
    scale_out[0:64, :] = jnp.where(pick, mm(high, spread), 0.0).astype(BF)
    scale_out[64:128, :] = jnp.where(pick, mm(low, spread), 0.0).astype(BF)


def dispatch_body(pick, n0, n1, n2, n3, out):
    rows = jnp.concatenate([n0[...], n1[...], n2[...], n3[...]], axis=0)
    choose = pick[...]
    for n in range(0, 2048, 512):
        out[:, n : n + 512] = mm(choose, rows[:, n : n + 512]).astype(BF)


def combine_body(scale, rows, p0, p1, p2, p3):
    for n in range(0, 2048, 512):
        part = rows[:, n : n + 512]
        total = mm(scale[...], part)
        total = total[:64, :] + total[64:, :]
        p0[:, n : n + 512] = total[0:16]
        p1[:, n : n + 512] = total[16:32].astype(BF)
        p2[:, n : n + 512] = total[32:48].astype(BF)
        p3[:, n : n + 512] = total[48:64].astype(BF)


def final_body(stream, p0, p1, p2, p3, out):
    total = p0[...] + p1[...].astype(F32) + p2[...].astype(F32) + p3[...].astype(F32)
    out[...] = (stream[...].astype(F32) + total).astype(BF)


def shifted(array, axis, size, by):
    return lax.ppermute(array, axis, [(i, (i + by) % size) for i in range(size)])


def shape(dims, dtype):
    return jax.ShapeDtypeStruct(dims, dtype)


def local(
    query_rows,
    key_rows,
    value_rows,
    output_gate,
    log_decay,
    write_rate,
    doc_start,
    state_in,
    head_gain,
    out_weight,
    residual,
    post_gain,
    expert_ids,
    expert_scale,
    w_gate_up,
    w_down,
):
    weights = [out_weight] + [shifted(out_weight, "x", 4, k) for k in (1, 2, 3)]

    big = shape((512, C), F32)
    erase, update, dr, start, prefix, own, sent = call(
        prep_body,
        (big, big, big, big, shape((3, 256, C), F32), shape((256, C), F32), shape((256, C), BF)),
        5,
        2_000_000_000,
        scratch=[
            pltpu.VMEM((512, C), BF),
            pltpu.VMEM((512, C), BF),
            pltpu.VMEM((1, 512), F32),
            pltpu.VMEM((1, 512), F32),
            pltpu.VMEM((1, 512), jnp.int32),
            pltpu.SemaphoreType.DMA((5,)),
        ],
        space=pltpu.HBM,
    )(
        *[
            pltpu.with_memory_space_constraint(a, pltpu.HBM)
            for a in (key_rows, value_rows, log_decay, write_rate, doc_start.reshape(1, 512))
        ]
    )
    other = shifted(sent, "c", 2, 1)
    pair = call(pair_body, shape((256, C), BF), 2, 50_000_000)(own, other)
    near, mid, far = [
        lax.ppermute(pair, "y", [(i, i + k) for i in range(4 - k)]) for k in (1, 2, 3)
    ]
    lead, rest = call(local_out_body, (big, big), 7, 1_000_000_000)(
        query_rows, key_rows, erase, update, dr, start, prefix
    )
    slab = shape((128, C), BF)
    slabs = call(
        gate_body,
        (slab, slab, slab, slab),
        9,
        400_000_000,
        scratch=[pltpu.VMEM((32, 16, C), BF)],
    )(
        lead,
        rest,
        output_gate,
        head_gain.reshape(1, C),
        state_in.reshape(C, C),
        near,
        mid,
        far,
        other,
    )
    moved = {k: shifted(slabs[k], "x", 4, k) for k in (2, 1, 3)}
    gated = [slabs[0], moved[1], moved[2], moved[3]]
    partial = call(project_body, shape((8, 16, 2048 + C), BF), 10, 400_000_000)(
        *gated, *weights, expert_ids, expert_scale
    )
    parts = lax.all_to_all(partial, ("zh", "zl"), 0, 0, tiled=True)
    row_block = shape((16, 2048), BF)
    stream, normed = call(stream_body, (row_block, row_block), 3, 10_000_000)(
        parts, residual, post_gain.reshape(1, 2048)
    )
    gathered = [normed] + [shifted(normed, "zh", 4, k) for k in ORDER]
    pick, scales = call(
        route_body,
        (shape((512, 64), BF), shape((128, 512), BF)),
        1,
        100_000_000,
    )(parts)
    outgoing = call(dispatch_body, shape((512, 2048), BF), 5, 200_000_000)(pick, *gathered)
    axes = ("y", "c", "zl", "x")
    arrived = lax.all_to_all(outgoing.reshape(64, 8, 2048), axes, 0, 0, tiled=True)
    flat = arrived.reshape(512, 2048)
    both = jnp.dot(flat, w_gate_up[0], preferred_element_type=F32)
    hidden = (jax.nn.silu(both[:, :512]) * both[:, 512:]).astype(BF)
    result = jnp.dot(hidden, w_down[0], preferred_element_type=F32).astype(BF)
    returned = lax.all_to_all(result.reshape(64, 8, 2048), axes, 0, 0, tiled=True)
    p0, p1, p2, p3 = call(
        combine_body,
        (shape((16, 2048), F32), row_block, row_block, row_block),
        2,
        300_000_000,
    )(scales, returned.reshape(512, 2048))
    back = [shifted(p, "zh", 4, -k) for k, p in zip(ORDER, (p1, p2, p3))]
    return call(final_body, row_block, 5, 1_000_000)(stream, p0, *back)


def solution(mesh):
    torus = Mesh(mesh.devices.reshape(4, 2, 4, 2, 4), ("y", "c", "zh", "zl", "x"))
    seq = ("y", "c")
    exp = ("zh", "zl", "x")
    every = seq + exp
    return jax.shard_map(
        local,
        mesh=torus,
        in_specs=(
            P(seq, exp),
            P(seq, exp),
            P(seq, exp),
            P(seq, exp),
            P(exp, seq),
            P(exp, seq),
            P(seq),
            P(exp, None, None),
            P(),
            P(exp, None),
            P(every, None),
            P(),
            P(every, None),
            P(every, None),
            P(every, None, None),
            P(every, None, None),
        ),
        out_specs=P(every, None),
        check_vma=False,
    )
```
